128 devices in a mesh: lat: 8 (over y_lo, x), lon: 16 (over y_hi, z, core).
Axes of the slice: x: 4, y: 4 (y_hi: 2, y_lo: 2; y = y_hi * 2 + y_lo), z: 4, core: 2. Of those that a mesh axis runs over, the one named last changes fastest.
Arguments:
- control: float32 [64, 128, 16384], P(None, 'lat', 'lon'), may hold values from -6 to 6
- vert_sqrt: float32 [64, 64], replicated, may hold values from -0.75 to 0.75
- kappa_lat: float32 [128, 16384], P('lat', 'lon'), may hold values from 0.12 to 0.48
- kappa_lon: float32 [128, 16384], P('lat', 'lon'), may hold values from 0.12 to 0.48
- obs_owner: int32 [131072, 1], P(('lat', 'lon')), may hold values from 0 to 127; in each aligned block of 1024 rows (0 to 1023, 1024 to 2047, ...) at most 16 rows name the same one
- obs_cell: int32 [131072], P(('lat', 'lon')), may hold values from 0 to 16383
- obs_weights: bfloat16 [64, 131072], P(None, ('lat', 'lon')), may hold values from -0.75 to 0.75
- obs_value: bfloat16 [131072], P(('lat', 'lon')), may hold values from -6 to 6
- obs_rinv: bfloat16 [131072], P(('lat', 'lon')), may hold values from 10 to 100
- obs_count: int32 [128], P(('lat', 'lon')), may hold values from 768 to 1024, as said below
Outputs:
- gradient: float32 [64, 128, 16384], P(None, 'lat', 'lon')
The draws below stay inside these ranges and needn't reach their ends.
Inputs may be any that keep to these rules, and one draw needn't show every extreme that they name: `obs_owner`: tile t is the device at lat index t // 16 and lon index t % 16. Among the 1024 rows of one device, live or not, no tile is named more than 16 times. Row-major cell of the owner tile: row obs_cell // 1024, column obs_cell % 1024. The first obs_count[d] rows of device d are live; on some device all 1024 rows are live.
All inputs are finite; a program needn't handle non-finite values.
Results may differ from the reference program's by a relative error of at most 0.0003.
Values may be sent and summed in bfloat16 or wider, within the bound.
A program may use at most 128 MiB of HBM per device.

```python
import math
import jax
import jax.numpy as jnp
import numpy as np
from jax import lax

LEV = 64
CLAT = 16
CLON = 1024
FSTEPS = 4
OBS_DEV = 1024
NLAT = 128
NLON = 16384
OBS_TOTAL = 131072
CAP = 16
N_LAT = 8
N_LON = 16


def draw_obs_count(key, part):
    first_key, second_key = jax.random.split(jax.random.fold_in(key, 17))
    devices = N_LAT * N_LON
    dropped = jax.random.randint(first_key, (devices,), 0, OBS_DEV // 4 + 1)
    chosen = jax.random.randint(second_key, (), 0, devices)
    counts = jnp.where(jnp.arange(devices) == chosen, OBS_DEV, OBS_DEV - dropped)
    return counts.astype(jnp.int32)


def place_ends(entries, key, smallest, high):
    longest = entries.shape.index(max(entries.shape))
    spots = []
    for shift in (0, 1):
        where = [jax.random.randint(jax.random.fold_in(key, axis), (), 0, length) for axis, length in enumerate(entries.shape)]
        where[longest] = (where[longest] + shift) % entries.shape[longest]
        spots.append(tuple(where))
    return entries.at[spots[0]].set(smallest).at[spots[1]].set(high)


def block_scale(rng, extent, cuts, least, largest):
    def one(axis_at, parts):
        heights = jax.random.uniform(jax.random.fold_in(jax.random.fold_in(rng, 6), axis_at), (parts,), jnp.float32, least / len(cuts), largest / len(cuts))
        return jnp.repeat(jnp.exp(heights), extent[axis_at] // parts).reshape((-1,) + (1,) * (len(extent) - axis_at - 1))

    loudness = one(*cuts[0])
    for cut in cuts[1:]:
        loudness = loudness * one(*cut)
    return loudness


def assign_block(rng, own, number, rows, amount, top, most, lean):
    order = jax.random.permutation(rng, amount)
    packed, common = shares(amount, rows * top, most, lean, True), shares(amount, rows * top, most, lean, False)
    places = jnp.arange(amount)

    def named(lengths, offset_by):
        used = int((lengths > 0).sum())
        fixed = max(1, used // 4)
        passed = fixed + (places - fixed + offset_by * (used - fixed)) % max(1, amount - fixed)
        return jnp.zeros((amount,), jnp.int32).at[order[jnp.where(places < fixed, places, passed)]].set(jnp.asarray(lengths, jnp.int32))

    lengths = jnp.where(number % 4 == 0, named(packed, number // 4), named(common, number - number // 4 - 1))
    mixed = jax.random.permutation(jax.random.fold_in(own, 3), amount)
    giver, sink = mixed[0:amount // 2 * 2:2], mixed[1:amount // 2 * 2:2]
    margin = jnp.minimum(lengths[giver] - 1, most - lengths[sink]) // 2
    margin = jnp.where((giver == order[0]) | (sink == order[0]) | (lengths[sink] == 0), 0, jnp.maximum(margin, 0))
    passed = jax.random.randint(jax.random.fold_in(own, 4), (amount // 2,), 0, 1 << 20) % (margin + 1)
    lengths = lengths.at[giver].add(-passed).at[sink].add(passed)
    labels = jnp.searchsorted(jnp.cumsum(lengths), jnp.arange(rows * top), side="right").astype(jnp.int32)
    listing = labels.reshape(top, rows).T
    listing = listing[jax.random.permutation(jax.random.fold_in(own, 1), rows)]
    offset_by = jax.random.randint(jax.random.fold_in(own, 2), (rows, 1), 0, top)
    return jnp.take_along_axis(listing, (jnp.arange(top)[None, :] + offset_by) % top, axis=1)


def shares(amount, total, bound, slope, full):
    loads = [(1 << 20) // math.isqrt(grade ** slope) + 1 for grade in range(1, amount + 1)]
    largest = bound if full else min(bound, max(-(-total // amount), total * loads[0] // sum(loads)))
    least = 1 if total - largest >= amount - 1 else 0
    given, spare = [largest] + [least] * (amount - 1), total - largest - least * (amount - 1)
    while spare > 0:
        free = [i for i in range(1, amount) if given[i] < largest] or [i for i in range(1, amount) if given[i] < bound]
        mass, remaining = sum([loads[i] for i in free]), spare
        for i in free:
            more = min(bound - given[i], max(1, remaining * loads[i] // mass), spare)
            given[i] = given[i] + more
            spare = spare - more
    return np.array(given)


def bell_draw(key, dims, width, reach, pieces=(), kind=jnp.bfloat16):
    array = width * jax.random.normal(key, dims, jnp.float32)
    if pieces:
        array = array * block_scale(key, dims, pieces, -0.22, 0.18)
    return jnp.clip(array, -reach, reach).astype(kind)


def setup_inputs(seed: int = 0) -> dict:
    streams_of = jax.random.split(jax.random.key(seed), 11)
    control = bell_draw(streams_of[0], (LEV, NLAT, NLON), 1.0, 6.0, ((1, 8), (2, 16)), jnp.float32)
    vert_sqrt = bell_draw(streams_of[1], (LEV, LEV), LEV ** -0.5, 0.75, (), jnp.float32)
    kappa_lat = jnp.clip(jnp.exp(math.log(0.48) - 1.3862944 * jax.random.uniform(streams_of[2], (NLAT, NLON), jnp.float32) ** block_scale(streams_of[2], (NLAT, NLON), ((0, 8), (1, 16)), -0.2, 0.2)), 0.12, 0.48)
    kappa_lon = jnp.clip(jnp.exp(math.log(0.48) - 1.3862944 * jax.random.uniform(streams_of[3], (NLAT, NLON), jnp.float32) ** block_scale(streams_of[3], (NLAT, NLON), ((0, 8), (1, 16)), -0.2, 0.2)), 0.12, 0.48)
    obs_owner_keys = jax.random.split(jax.random.fold_in(streams_of[4], 1), OBS_TOTAL // OBS_DEV)
    obs_owner_turns = jax.random.permutation(jax.random.fold_in(streams_of[4], 3), OBS_TOTAL // OBS_DEV)
    obs_owner = jax.vmap(lambda own, number: assign_block(jax.random.fold_in(streams_of[4], 2), own, number, OBS_DEV, N_LAT * N_LON, 1, CAP, 2))(obs_owner_keys, obs_owner_turns).reshape((OBS_TOTAL, 1))
    obs_cell = place_ends(jax.random.randint(streams_of[5], (OBS_TOTAL,), 0, CLAT * CLON), jax.random.fold_in(streams_of[5], 1), 0, (CLAT * CLON) - 1).astype(jnp.int32)
    obs_weights = bell_draw(streams_of[6], (LEV, OBS_TOTAL), LEV ** -0.5, 0.75, ((1, 128),))
    obs_value = bell_draw(streams_of[7], (OBS_TOTAL,), 1.0, 6.0, ((0, 128),))
    obs_rinv = jnp.clip(jnp.exp(math.log(100.0) - 2.3025851 * jax.random.uniform(streams_of[8], (OBS_TOTAL,), jnp.float32) ** block_scale(streams_of[8], (OBS_TOTAL,), ((0, 128),), -0.2, 0.2)), 10.0, 100.0).astype(jnp.bfloat16)
    obs_count = draw_obs_count(jax.random.fold_in(streams_of[10], 71), 0)
    return dict(control=control, vert_sqrt=vert_sqrt, kappa_lat=kappa_lat, kappa_lon=kappa_lon, obs_owner=obs_owner, obs_cell=obs_cell, obs_weights=obs_weights, obs_value=obs_value, obs_rinv=obs_rinv, obs_count=obs_count)


def lat_forward(values, coeff):
    padded = jnp.pad(values, ((0, 0), (1, 1), (0, 0)))
    return values + coeff * (padded[:, :-2] + padded[:, 2:] - 2.0 * values)

def lon_forward(values, coeff):
    return values + coeff * (jnp.roll(values, 1, 2) + jnp.roll(values, -1, 2) - 2.0 * values)

def lat_adjoint(values, coeff):
    weighted = coeff * values
    padded = jnp.pad(weighted, ((0, 0), (1, 1), (0, 0)))
    return values + (padded[:, :-2] + padded[:, 2:] - 2.0 * weighted)

def lon_adjoint(values, coeff):
    weighted = coeff * values
    return values + (jnp.roll(weighted, 1, 2) + jnp.roll(weighted, -1, 2) - 2.0 * weighted)

def reference(control, vert_sqrt, kappa_lat, kappa_lon, obs_owner, obs_cell, obs_weights, obs_value, obs_rinv, obs_count):
    precise = lax.Precision.HIGHEST
    state = jnp.einsum('lm,mij->lij', vert_sqrt, control, precision=precise)
    for sweep in range(FSTEPS):
        state = lat_forward(state, kappa_lat)
    for sweep in range(FSTEPS):
        state = lon_forward(state, kappa_lon)
    owner_tile = obs_owner[:, 0]
    grid_row = owner_tile // N_LON * CLAT + obs_cell // CLON
    grid_col = owner_tile % N_LON * CLON + obs_cell % CLON
    flat_cell = (grid_row * NLON + grid_col).astype(jnp.int32)
    flat_state = state.reshape(LEV, NLAT * NLON)
    weights = obs_weights.astype(jnp.float32)
    modelled = lax.optimization_barrier(jnp.sum(weights * flat_state[:, flat_cell], axis=0))
    row_index = jnp.arange(OBS_TOTAL, dtype=jnp.int32)
    live = row_index % OBS_DEV < obs_count[(row_index // OBS_DEV).astype(jnp.int32)]
    misfit = jnp.where(live, obs_rinv.astype(jnp.float32) * (modelled - obs_value.astype(jnp.float32)), jnp.zeros_like(modelled))
    forcing = jnp.zeros((LEV, NLAT * NLON), jnp.float32).at[:, flat_cell].add(weights * misfit[None, :])
    adjoint = forcing.reshape(LEV, NLAT, NLON)
    for sweep in range(FSTEPS):
        adjoint = lon_adjoint(adjoint, kappa_lon)
    for sweep in range(FSTEPS):
        adjoint = lat_adjoint(adjoint, kappa_lat)
    return control + jnp.einsum('lm,lij->mij', vert_sqrt, adjoint, precision=precise)
```

```python
import functools

import jax
import jax.numpy as jnp
from jax import lax
from jax.experimental import pallas as pl
from jax.experimental.pallas import tpu as pltpu
from jax.sharding import PartitionSpec as P

STEPS = 4
CAP = 16
GROUPS = 8
LANES = 128
VMEM_BYTES = 62 * 1024 * 1024
F32 = jnp.float32
BF16 = jnp.bfloat16
I32 = jnp.int32


def dot(a, b):
    return jnp.dot(a, b, preferred_element_type=F32)


def dot_nt(a, b):
    return lax.dot_general(a, b, (((1,), (1,)), ((), ())), preferred_element_type=F32)


def split(x):
    high = x.astype(BF16)
    return high, (x - high.astype(F32)).astype(BF16)


def iota(shape, axis):
    return lax.broadcasted_iota(I32, shape, axis)


def pack_kernel(count_ref, owner_ref, cell_ref, value_ref, rinv_ref, w_ref, wsend_ref, ssend_ref):
    devices = ssend_ref.shape[0]
    levels, total = w_ref.shape
    slot_id = iota((1, total), 1)
    live = slot_id < count_ref[0]
    owner = jnp.where(live, owner_ref[...], -1)
    cell = cell_ref[...]
    row = cell >> 10
    hot = iota((devices, total), 0) == owner
    classes = (row < STEPS, (row >= STEPS) & (row < 12), row >= 12)
    tables = [(hot & c).astype(F32) for c in classes]
    tri = (iota((total, total), 0) < iota((total, total), 1)).astype(F32).astype(BF16)
    stack = jnp.concatenate(tables, 0)
    earlier = dot(stack.astype(BF16), tri)
    first = jnp.sum(tables[0], axis=1, keepdims=True)
    place = (
        tables[0] * earlier[:devices]
        + tables[1] * (first + earlier[devices : 2 * devices])
        + tables[2] * ((CAP - 1.0) - earlier[2 * devices :])
    )
    slot = jnp.sum(place, axis=0, keepdims=True).astype(I32)
    dest = jnp.where(live, owner * CAP + slot, -1)
    weights = w_ref[...]
    blank = jnp.zeros_like(weights)
    lower = jnp.concatenate([weights, blank], 0)
    upper = jnp.concatenate([blank, weights], 0)
    rows = min(128, devices * 8)
    for chunk in range(devices * 8 // rows):
        r = iota((rows, total), 0) + chunk * rows
        base = (r >> 3) * CAP + (r & 7)
        p0 = (base == dest).astype(F32).astype(BF16)
        p1 = (base + 8 == dest).astype(F32).astype(BF16)
        out = dot_nt(p0, lower) + dot_nt(p1, upper)
        wsend_ref[pl.ds(chunk * (rows // 8), rows // 8)] = out.reshape(rows // 8, 8, LANES).astype(BF16)
    k = iota((LANES, total), 0)
    kind = k >> 4
    match = (k & 15) == slot
    val = jnp.where(
        kind == 0,
        value_ref[...].astype(F32),
        jnp.where(
            kind == 1,
            rinv_ref[...].astype(F32),
            jnp.where(kind == 2, (cell >> 7).astype(F32), (cell & 127).astype(F32)),
        ),
    )
    table = jnp.where(match & (kind < 4), val, 0.0).astype(BF16)
    scal = dot_nt(hot.astype(F32).astype(BF16), table)
    ssend_ref[...] = scal.reshape(devices, 1, LANES)


def pack(count, owner, cell, value, rinv, weights, devices):
    total = owner.shape[1]
    vm = pl.BlockSpec(memory_space=pltpu.VMEM)
    return pl.pallas_call(
        pack_kernel,
        out_shape=(
            jax.ShapeDtypeStruct((devices, 8, LANES), BF16),
            jax.ShapeDtypeStruct((devices, 1, LANES), F32),
        ),
        in_specs=[pl.BlockSpec(memory_space=pltpu.SMEM)] + [vm] * 5,
        out_specs=(vm, vm),
        compiler_params=pltpu.CompilerParams(vmem_limit_bytes=VMEM_BYTES),
        name="pack",
    )(count, owner, cell, value, rinv, weights)


def exchange_kernel(n_lat, n_lon, w_ref, s_ref, wo_ref, so_ref, w_send, w_recv, s_send, s_recv, own_sem):
    devices = n_lat * n_lon
    me = lax.axis_index("lat") * n_lon + lax.axis_index("lon")
    barrier = pltpu.get_barrier_semaphore()

    def peer(step):
        t = lax.rem(me + step, devices)
        return t, (t // n_lon, lax.rem(t, n_lon))

    def greet(step, carry):
        _, where = peer(step)
        pl.semaphore_signal(barrier, inc=1, device_id=where, device_id_type=pl.DeviceIdType.MESH)
        return carry

    lax.fori_loop(1, devices, greet, 0)
    own = (
        pltpu.make_async_copy(w_ref.at[me], wo_ref.at[me], own_sem.at[0]),
        pltpu.make_async_copy(s_ref.at[me], so_ref.at[me], own_sem.at[1]),
    )
    for c in own:
        c.start()
    pl.semaphore_wait(barrier, devices - 1)

    def send(step, carry):
        t, where = peer(step)
        pltpu.make_async_remote_copy(
            src_ref=w_ref.at[t], dst_ref=wo_ref.at[me], send_sem=w_send, recv_sem=w_recv,
            device_id=where, device_id_type=pl.DeviceIdType.MESH,
        ).start()
        pltpu.make_async_remote_copy(
            src_ref=s_ref.at[t], dst_ref=so_ref.at[me], send_sem=s_send, recv_sem=s_recv,
            device_id=where, device_id_type=pl.DeviceIdType.MESH,
        ).start()
        return carry

    lax.fori_loop(1, devices, send, 0)
    for c in own:
        c.wait()
    part = pl.ds(0, devices - 1)
    for src, dst, send_sem, recv_sem in ((w_ref, wo_ref, w_send, w_recv), (s_ref, so_ref, s_send, s_recv)):
        pltpu.make_async_copy(src.at[part], src.at[part], send_sem).wait()
        pltpu.make_async_copy(dst.at[part], dst.at[part], recv_sem).wait()


def exchange(wsend, ssend, n_lat, n_lon):
    vm = pl.BlockSpec(memory_space=pltpu.VMEM)
    return pl.pallas_call(
        functools.partial(exchange_kernel, n_lat, n_lon),
        out_shape=(
            jax.ShapeDtypeStruct(wsend.shape, wsend.dtype),
            jax.ShapeDtypeStruct(ssend.shape, ssend.dtype),
        ),
        in_specs=[vm, vm],
        out_specs=(vm, vm),
        scratch_shapes=[
            pltpu.SemaphoreType.DMA,
            pltpu.SemaphoreType.DMA,
            pltpu.SemaphoreType.DMA,
            pltpu.SemaphoreType.DMA,
            pltpu.SemaphoreType.DMA((2,)),
        ],
        compiler_params=pltpu.CompilerParams(collective_id=0, has_side_effects=True),
        name="exchange",
    )(wsend, ssend)


def tile_rows(i, block):
    return pl.ds((i // 8) * 64 + block * 8 + i % 8, 64, stride=128)


def to_tiles(x):
    levels, rows, cols = x.shape
    x = x.reshape(levels, rows // 8, 8, cols // LANES, LANES).transpose(0, 1, 3, 2, 4)
    return x.reshape(-1, LANES)


def from_tiles(x, shape):
    levels, rows, cols = shape
    x = x.reshape(levels, rows // 8, cols // LANES, 8, LANES).transpose(0, 1, 3, 2, 4)
    return x.reshape(shape)


def turn_in(load, store):
    for p in range(4):
        t = jnp.concatenate([load(p), load(p + 4)], 0).T
        store(2 * p, t[:64])
        store(2 * p + 1, t[64:])


def wrap_low(v, edge):
    rolled = pltpu.roll(v, 1, 0)
    sub = iota(v.shape, 0)
    lane = iota(v.shape, 1)
    return jnp.where(sub == 0, jnp.where(lane < 64, edge, pltpu.roll(rolled, 64, 1)), rolled)


def wrap_high(v, edge):
    rolled = pltpu.roll(v, GROUPS - 1, 0)
    sub = iota(v.shape, 0)
    lane = iota(v.shape, 1)
    return jnp.where(sub == GROUPS - 1, jnp.where(lane >= 64, edge, pltpu.roll(rolled, 64, 1)), rolled)


def spread_coeffs(kext_ref, west_ref, east_ref, kt, klat, klon):
    ext = klat.shape[0]
    wide = klat.shape[1]

    def store(g, t):
        kt[pl.ds(STEPS * 8 + g, 64, stride=8), :] = t

    turn_in(lambda p: kext_ref[:, p * LANES : (p + 1) * LANES], store)
    for t in range(STEPS):
        v = kt[pl.ds((64 + t) * 8, 8), :]
        kt[pl.ds(t * 8, 8), :] = wrap_low(v, jnp.broadcast_to(west_ref[pl.ds(t, 1), :], (8, LANES)))
        v = kt[pl.ds((4 + t) * 8, 8), :]
        kt[pl.ds((68 + t) * 8, 8), :] = wrap_high(v, jnp.broadcast_to(east_ref[pl.ds(t, 1), :], (8, LANES)))
    both = jnp.concatenate(list(split(kt[...])), 1)
    r = iota((256, 256), 0)
    c = iota((256, 256), 1)
    same = ((r >> 6) & 1) == ((c >> 6) & 1)
    want = (r & 63) - 32 * (c >> 7)

    def one(i, carry):
        pick = (same & (want == i)).astype(F32).astype(BF16)
        out = dot(both, pick)
        klat[i] = out[:, :LANES]
        klon[i] = out[:, LANES:]
        return carry

    lax.fori_loop(0, ext, one, 0)


def forward_kernel(c_ref, west_ref, east_ref, kext_ref, kwest_ref, keast_ref, out_ref, s0, s1, kt, klat, klon):
    rows = west_ref.shape[0]
    ext = rows + 2 * STEPS
    wide = 64 + 2 * STEPS

    def turn(i, carry):
        def store(g, t):
            s0[pl.ds((i * wide + STEPS) * 8 + g, 64, stride=8), :] = t

        turn_in(lambda p: c_ref[tile_rows(i, p), :], store)
        for t in range(STEPS):
            v = s0[pl.ds(pl.multiple_of((i * wide + 64 + t) * 8, 8), 8), :]
            s0[pl.ds(pl.multiple_of((i * wide + t) * 8, 8), 8), :] = wrap_low(
                v, jnp.broadcast_to(west_ref[i, pl.ds(t, 1), :], (8, LANES)))
            v = s0[pl.ds(pl.multiple_of((i * wide + 4 + t) * 8, 8), 8), :]
            s0[pl.ds(pl.multiple_of((i * wide + 68 + t) * 8, 8), 8), :] = wrap_high(
                v, jnp.broadcast_to(east_ref[i, pl.ds(t, 1), :], (8, LANES)))
        return carry

    lax.fori_loop(0, rows, turn, 0)
    spread_coeffs(kext_ref, kwest_ref, keast_ref, kt, klat, klon)

    def lat(q, carry):
        at = pl.ds(pl.multiple_of(q * 8, 8), 8)
        x = {STEPS + i: s0[pl.ds(pl.multiple_of((i * wide + q) * 8, 8), 8), :] for i in range(rows)}
        k = [klat[i, at, :] for i in range(ext)]
        for step in range(STEPS):
            lo, hi = min(x), max(x)
            d = {}
            for i in range(lo - 1, hi + 1):
                if i < lo:
                    d[i] = x[lo]
                elif i == hi:
                    d[i] = -x[hi]
                else:
                    d[i] = x[i + 1] - x[i]
            new = {}
            for i in range(lo - 1, hi + 2):
                if i < lo:
                    new[i] = k[i] * x[lo]
                elif i > hi:
                    new[i] = k[i] * x[hi]
                else:
                    new[i] = x[i] + k[i] * (d[i] - d[i - 1])
            x = new
        for i in range(ext):
            s1[i, at, :] = x[i]
        return carry

    lax.fori_loop(0, wide, lat, 0)

    def lon(i, carry):
        stages = [[] for _ in range(STEPS + 1)]
        diffs = [[] for _ in range(STEPS)]
        coef = []
        for q in range(wide):
            stages[0].append(s1[i, q * 8 : q * 8 + 8, :])
            coef.append(klon[i, q * 8 : q * 8 + 8, :])
            for s in range(STEPS):
                x = stages[s]
                n = len(x)
                if n >= 2:
                    diffs[s].append(x[n - 1] - x[n - 2])
                if n >= 3:
                    mid = n - 2
                    stages[s + 1].append(x[mid] + coef[mid + s] * (diffs[s][-1] - diffs[s][-2]))
                    if s == STEPS - 1:
                        out_ref[i, mid - 1] = stages[STEPS][-1]
        return carry

    lax.fori_loop(0, ext, lon, 0)


def forward(control2, west, east, kext, kwest, keast):
    rows = west.shape[0]
    ext = rows + 2 * STEPS
    wide = 64 + 2 * STEPS
    vm = pl.BlockSpec(memory_space=pltpu.VMEM)
    return pl.pallas_call(
        forward_kernel,
        out_shape=jax.ShapeDtypeStruct((ext, 64, 8, LANES), F32),
        in_specs=[vm] * 6,
        out_specs=vm,
        scratch_shapes=[
            pltpu.VMEM((rows * wide * 8, LANES), F32),
            pltpu.VMEM((ext, wide * 8, LANES), F32),
            pltpu.VMEM((wide * 8, LANES), F32),
            pltpu.VMEM((ext, wide * 8, LANES), F32),
            pltpu.VMEM((ext, wide * 8, LANES), F32),
        ],
        compiler_params=pltpu.CompilerParams(vmem_limit_bytes=VMEM_BYTES),
        cost_estimate=pl.CostEstimate(flops=200000000, bytes_accessed=40000000, transcendentals=0),
        name="forward_filter",
    )(control2, west, east, kext, kwest, keast)


def level_mix(w_ref, mix_ref, u):
    devices = w_ref.shape[0]
    w = w_ref[...].astype(F32).reshape(devices * 8, LANES).astype(BF16)
    high, low = split(mix_ref[...])
    both = dot(jnp.concatenate([w, w], 1), jnp.concatenate([high, low], 0))
    u[0] = both[:, :LANES]
    u[1] = both[:, LANES:]


def list_fields(s_ref):
    devices = s_ref.shape[0]
    value = s_ref[...].reshape(devices, LANES)
    rinv = pltpu.roll(value, LANES - 16, 1)
    cell = (pltpu.roll(value, LANES - 32, 1) * 128.0 + pltpu.roll(value, LANES - 48, 1)).astype(I32)
    row = cell >> 10
    col = cell & 1023
    where = (col & 63) * 8 + ((col >> 6) & 7)
    valid = (rinv > 0.5) & (iota(value.shape, 1) < CAP)
    return value, rinv, row, where, col >> 9, valid


def count_max(mask, weight):
    return jnp.max(jnp.where(mask, weight, 0), axis=1, keepdims=True)


def relevant(row, valid):
    return (valid, valid & (row >= 12), valid & (row < STEPS))


def tables(number, row, where, valid):
    lane = iota(row.shape, 1)
    front = valid & (row < 12)
    back = valid & (row >= 12)
    slot = lane + 1
    depth = CAP - lane
    need = relevant(row, valid)[number]
    shift = (STEPS, -12, 20)[number]
    gather = jnp.where(need, (row + shift) * 512 + where, 0)
    if number == 0:
        first = jnp.where(front, row * 512 + where, 12 * 512)
        second = jnp.where(back, (row - 12) * 512 + where, 4 * 512)
        nf = count_max(front, slot)
        nb = count_max(back, depth)
        mid = jnp.maximum(nf, nb - 4)
        late = jnp.maximum(nf - 4, nb)
        n0, n1, n2, n3 = mid, late, nf, nb
    elif number == 1:
        first = jnp.where(need, (row - 12) * 512 + where, 4 * 512)
        second = first
        n0 = n1 = n2 = n3 = count_max(need, depth)
    else:
        first = jnp.where(need, row * 512 + where, 4 * 512)
        second = first
        n0 = n1 = n2 = n3 = count_max(need, slot)
    out = jnp.where(lane < 16, gather, 0)
    out = jnp.where((lane >= 16) & (lane < 32), pltpu.roll(first, 16, 1), out)
    out = jnp.where((lane >= 32) & (lane < 48), pltpu.roll(second, 32, 1), out)
    for at, n in ((48, n0), (49, n1), (50, n2), (51, n3)):
        out = jnp.where(lane == at, n, out)
    return out


def gather_kernel(field_ref, mix_ref, *refs):
    w_refs, s_refs = refs[0:3], refs[3:6]
    part_ref, table_ref = refs[6:8]
    u, picked, smem, sem = refs[8:]
    devices = s_refs[0].shape[0]
    info = []
    for n in range(3):
        value, rinv, row, where, gh, valid = list_fields(s_refs[n])
        table_ref[n] = tables(n, row, where, valid)
        info.append((gh, relevant(row, valid)[n]))
    copy = pltpu.make_async_copy(table_ref, smem, sem)
    copy.start()
    for n in range(3):
        level_mix(w_refs[n], mix_ref, u.at[n])
    copy.wait()

    def fetch(n, s, slots):
        for k in slots:
            r = smem[n, s, k]
            picked[n, k, pl.ds(s, 1), :] = field_ref[pl.ds(r, 1), :]

    def source(s, carry):
        fetch(0, s, (0, 1, 2, 3, 12, 13, 14, 15))
        fetch(1, s, (12, 13, 14, 15))
        fetch(2, s, (0, 1, 2, 3))
        mid, late = smem[0, s, 48], smem[0, s, 49]
        north, south = smem[1, s, 48], smem[2, s, 48]

        @pl.when(mid > 4)
        def _():
            fetch(0, s, (4, 5, 6, 7))

        @pl.when(late > 4)
        def _():
            fetch(0, s, (8, 9, 10, 11))

        @pl.when(north > 4)
        def _():
            fetch(1, s, range(12))

        @pl.when(south > 4)
        def _():
            fetch(2, s, range(4, 16))

        return carry

    lax.fori_loop(0, devices, source, 0)
    lane = iota((devices, LANES), 1)
    for n in range(3):
        gh, keep = info[n]
        gh = jnp.where(keep, gh, -1)
        total = jnp.zeros((devices, LANES), F32)
        for k in range(CAP):
            uk = u[n, k // 8, pl.ds(k % 8, devices, stride=8), :]
            sel = jnp.broadcast_to(gh[:, k : k + 1], uk.shape) == (lane >> 6)
            prod = jnp.where(sel, uk * picked[n, k], 0.0)
            total = jnp.where(lane == k, jnp.sum(prod, axis=1, keepdims=True), total)
        part_ref[n] = total


def gather(field, mix, w_lists, s_lists):
    devices = s_lists[0].shape[0]
    vm = pl.BlockSpec(memory_space=pltpu.VMEM)
    return pl.pallas_call(
        gather_kernel,
        out_shape=(
            jax.ShapeDtypeStruct((3, devices, LANES), F32),
            jax.ShapeDtypeStruct((3, devices, LANES), I32),
        ),
        in_specs=[vm] * 8,
        out_specs=(vm, vm),
        scratch_shapes=[
            pltpu.VMEM((3, 2, devices * 8, LANES), F32),
            pltpu.VMEM((3, CAP, devices, LANES), F32),
            pltpu.SMEM((3, devices, LANES), I32),
            pltpu.SemaphoreType.DMA,
        ],
        compiler_params=pltpu.CompilerParams(vmem_limit_bytes=VMEM_BYTES),
        name="gather",
    )(field, mix, *w_lists, *s_lists)


def adjoint_kernel(part_ref, north_ref, south_ref, table_ref, mix_ref, *refs):
    w_refs, s_refs = refs[0:3], refs[3:6]
    kext_ref, kwest_ref, keast_ref, out_ref, west_ref, east_ref = refs[6:12]
    u, force, a_north, a_front, a_back, a_south, s1, kt, klat, klon = refs[12:]
    devices = s_refs[0].shape[0]
    rows = out_ref.shape[0]
    ext = rows + 2 * STEPS
    wide = 64 + 2 * STEPS
    for a in (a_north, a_front, a_back, a_south):
        size = a.shape[0] // 64

        def clear(i, carry, a=a):
            a[pl.ds(pl.multiple_of(i * 64, 64), 64), :] = jnp.zeros((64, LANES), F32)
            return carry

        lax.fori_loop(0, size, clear, 0)
    spread_coeffs(kext_ref, kwest_ref, keast_ref, kt, klat, klon)
    lane = iota((devices, LANES), 1)
    totals = (
        part_ref[0] + north_ref[1] + south_ref[1],
        part_ref[1] + north_ref[0],
        part_ref[2] + south_ref[0],
    )
    for n in range(3):
        level_mix(w_refs[n], mix_ref, u)
        value, rinv, row, where, gh, valid = list_fields(s_refs[n])
        misfit = rinv * (totals[n] - value)
        for k in range(CAP):
            uk = u[k // 8, pl.ds(k % 8, devices, stride=8), :]
            sel = jnp.broadcast_to(gh[:, k : k + 1], uk.shape) == (lane >> 6)
            force[n, k] = jnp.where(sel, uk * misfit[:, k : k + 1], 0.0)

    def add(a, n, s, k, at):
        r = table_ref[n, s, at + k]
        a[pl.ds(r, 1), :] += force[n, k, pl.ds(s, 1), :]

    def source(s, carry):
        for k in range(4):
            add(a_front, 0, s, k, 16)
            add(a_back, 0, s, CAP - 1 - k, 32)
            add(a_north, 1, s, CAP - 1 - k, 16)
            add(a_south, 2, s, k, 16)
        nf, nb = table_ref[0, s, 50], table_ref[0, s, 51]
        north, south = table_ref[1, s, 48], table_ref[2, s, 48]
        for g in range(1, 4):
            @pl.when(nf > 4 * g)
            def _(g=g):
                for k in range(4 * g, 4 * g + 4):
                    add(a_front, 0, s, k, 16)

        @pl.when(jnp.maximum(nb, jnp.maximum(north, south)) > 4)
        def _():
            for k in range(4, CAP):
                add(a_back, 0, s, CAP - 1 - k, 32)
                add(a_north, 1, s, CAP - 1 - k, 16)
                add(a_south, 2, s, k, 16)

        return carry

    lax.fori_loop(0, devices, source, 0)

    def lon(source, first, count):
        def one(i, carry):
            stages = [{} for _ in range(STEPS + 1)]
            k = {}
            h = [{} for _ in range(STEPS)]
            d = [{} for _ in range(STEPS)]

            def coef(q):
                if q not in k:
                    k[q] = klon[first + i, (q + STEPS) * 8 : (q + STEPS) * 8 + 8, :]
                return k[q]

            for q in range(-1, 64 + 2 * STEPS + 1):
                for s in range(STEPS):
                    lo, hi = -s, 63 + s
                    at = q - s
                    if s == 0 and lo <= at <= hi:
                        stages[0][at] = source[pl.ds(pl.multiple_of((i * 64 + at) * 8, 8), 8), :]
                    if lo <= at <= hi + 2:
                        if at == lo:
                            h[s][at] = coef(at) * stages[s][at]
                            d[s][at - 1] = h[s][at]
                            stages[s + 1][at - 1] = h[s][at]
                        else:
                            if at <= hi:
                                h[s][at] = coef(at) * stages[s][at]
                            if at <= hi:
                                d[s][at - 1] = h[s][at] - h[s][at - 1]
                            elif at == hi + 1:
                                d[s][at - 1] = -h[s][at - 1]
                            m = at - 1
                            if m <= hi:
                                stages[s + 1][m] = stages[s][m] + (d[s][m] - d[s][m - 1])
                            else:
                                stages[s + 1][m] = -d[s][m - 1]
            for q in range(-STEPS, 64 + STEPS):
                s1[first + i, (q + STEPS) * 8 : (q + STEPS) * 8 + 8, :] = stages[STEPS][q]
            return carry

        lax.fori_loop(0, count, one, 0)

    lon(a_north, 0, STEPS)
    lon(a_front, STEPS, 12)
    lon(a_back, rows, STEPS)
    lon(a_south, rows + STEPS, STEPS)

    def lat(q, carry):
        at = pl.ds(pl.multiple_of(q * 8, 8), 8)
        x = {i: s1[i, at, :] for i in range(ext)}
        k = [klat[i, at, :] for i in range(ext)]
        for step in range(STEPS):
            h = {i: k[i] * x[i] for i in x}
            lo, hi = min(x), max(x)
            d = {i: h[i + 1] - h[i] for i in range(lo, hi)}
            x = {i: x[i] + (d[i] - d[i - 1]) for i in range(lo + 1, hi)}
        for i in range(rows):
            s1[i, at, :] = x[STEPS + i]
        return carry

    lax.fori_loop(0, wide, lat, 0)

    def fold(i, carry):
        zero = jnp.zeros((8, LANES), F32)

        def body(q, carry):
            out_ref[i, q] = s1[i, pl.ds(pl.multiple_of((q + STEPS) * 8, 8), 8), :]
            return carry

        lax.fori_loop(STEPS, 64 - STEPS, body, 0, unroll=8)
        for t in range(STEPS):
            low = s1[i, t * 8 : t * 8 + 8, :]
            high = s1[i, (68 + t) * 8 : (68 + t) * 8 + 8, :]
            west_ref[i, pl.ds(t, 1), :] = low[0:1]
            east_ref[i, pl.ds(t, 1), :] = high[GROUPS - 1 :]
            out_ref[i, 60 + t] = s1[i, (64 + t) * 8 : (64 + t) * 8 + 8, :] + wrap_high(low, zero)
            out_ref[i, t] = s1[i, (4 + t) * 8 : (4 + t) * 8 + 8, :] + wrap_low(high, zero)
        return carry

    lax.fori_loop(0, rows, fold, 0)


def adjoint(part, north, south, table, mix, w_lists, s_lists, kext, kwest, keast, rows):
    devices = s_lists[0].shape[0]
    ext = rows + 2 * STEPS
    wide = 64 + 2 * STEPS
    vm = pl.BlockSpec(memory_space=pltpu.VMEM)
    return pl.pallas_call(
        adjoint_kernel,
        out_shape=(
            jax.ShapeDtypeStruct((rows, 64, 8, LANES), F32),
            jax.ShapeDtypeStruct((rows, STEPS, LANES), F32),
            jax.ShapeDtypeStruct((rows, STEPS, LANES), F32),
        ),
        in_specs=[vm] * 3 + [pl.BlockSpec(memory_space=pltpu.SMEM)] + [vm] * 10,
        out_specs=(vm, vm, vm),
        scratch_shapes=[
            pltpu.VMEM((2, devices * 8, LANES), F32),
            pltpu.VMEM((3, CAP, devices, LANES), F32),
            pltpu.VMEM((4 * 512 + 64, LANES), F32),
            pltpu.VMEM((12 * 512 + 64, LANES), F32),
            pltpu.VMEM((4 * 512 + 64, LANES), F32),
            pltpu.VMEM((4 * 512 + 64, LANES), F32),
            pltpu.VMEM((ext, wide * 8, LANES), F32),
            pltpu.VMEM((wide * 8, LANES), F32),
            pltpu.VMEM((ext, wide * 8, LANES), F32),
            pltpu.VMEM((ext, wide * 8, LANES), F32),
        ],
        compiler_params=pltpu.CompilerParams(vmem_limit_bytes=VMEM_BYTES),
        name="adjoint_filter",
    )(part, north, south, table, mix, *w_lists, *s_lists, kext, kwest, keast)


def finish_kernel(field_ref, west_ref, east_ref, c_ref, out_ref, s0):
    rows = west_ref.shape[0]
    lane = iota((1, LANES), 1)

    def turn(i, carry):
        def copy(q, c):
            s0[pl.ds(pl.multiple_of(q * 8, 8), 8), :] = field_ref[i, q]
            return c

        lax.fori_loop(0, 64, copy, 0, unroll=8)
        for t in range(STEPS):
            row = t * 8
            s0[row : row + 1, :] += jnp.where(lane < 64, west_ref[i, pl.ds(t, 1), :], 0.0)
            row = (60 + t) * 8 + GROUPS - 1
            s0[row : row + 1, :] += jnp.where(lane >= 64, east_ref[i, pl.ds(t, 1), :], 0.0)
        for p in range(4):
            t = jnp.concatenate(
                [s0[pl.ds(2 * p, 64, stride=8), :], s0[pl.ds(2 * p + 1, 64, stride=8), :]], 0
            ).T
            for gh in range(2):
                at = tile_rows(i, 4 * gh + p)
                out_ref[at, :] = c_ref[at, :] + t[gh * 64 : gh * 64 + 64]
        return carry

    lax.fori_loop(0, rows, turn, 0)


def finish(field, west, east, control2):
    vm = pl.BlockSpec(memory_space=pltpu.VMEM)
    return pl.pallas_call(
        finish_kernel,
        out_shape=jax.ShapeDtypeStruct(control2.shape, F32),
        in_specs=[vm] * 4,
        out_specs=vm,
        scratch_shapes=[pltpu.VMEM((64 * 8, LANES), F32)],
        compiler_params=pltpu.CompilerParams(vmem_limit_bytes=VMEM_BYTES),
        name="finish",
    )(field, west, east, control2)


def shifts(axis, periodic):
    count = lax.axis_size(axis)
    up = [(i, i + 1) for i in range(count - 1)] + ([(count - 1, 0)] if periodic else [])
    return up, [(b, a) for a, b in up]


def body(control, vert_sqrt, kappa_lat, kappa_lon, obs_owner, obs_cell, obs_weights, obs_value, obs_rinv, obs_count):
    levels, rows, cols = control.shape
    n_lat, n_lon = lax.axis_size("lat"), lax.axis_size("lon")
    devices = n_lat * n_lon
    total = obs_cell.shape[0]
    down, up = shifts("lat", False)
    eastward, westward = shifts("lon", True)

    wsend, ssend = pack(
        obs_count, obs_owner.reshape(1, total), obs_cell.reshape(1, total),
        obs_value.reshape(1, total), obs_rinv.reshape(1, total), obs_weights, devices,
    )
    kappa = jnp.stack([kappa_lat, kappa_lon])
    knorth = lax.ppermute(kappa[:, rows - STEPS :], "lat", down)
    ksouth = lax.ppermute(kappa[:, :STEPS], "lat", up)
    pad = jnp.zeros((2, 32 - rows - 2 * STEPS, cols), F32)
    kext = jnp.concatenate([knorth, kappa, ksouth, pad], 1).reshape(64, cols)
    edge_hi = jnp.concatenate([control[:, :, cols - STEPS :], kext[:, None, cols - STEPS :]], 1)
    edge_lo = jnp.concatenate([control[:, :, :STEPS], kext[:, None, :STEPS]], 1)
    from_west = lax.ppermute(edge_hi.transpose(1, 2, 0), "lon", eastward)
    from_east = lax.ppermute(edge_lo.transpose(1, 2, 0), "lon", westward)
    none = jnp.zeros_like(from_west)
    from_west = jnp.concatenate([from_west, none], 2)
    from_east = jnp.concatenate([none, from_east], 2)
    west, kwest = from_west[:rows], from_west[rows]
    east, keast = from_east[:rows], from_east[rows]
    control2 = to_tiles(control)

    w_own, s_own = exchange(wsend, ssend, n_lat, n_lon)
    w_north = lax.ppermute(w_own, "lat", down)
    s_north = lax.ppermute(s_own, "lat", down)
    w_south = lax.ppermute(w_own, "lat", up)
    s_south = lax.ppermute(s_own, "lat", up)
    w_lists = (w_own, w_north, w_south)
    s_lists = (s_own, s_north, s_south)

    field = forward(control2, west, east, kext, kwest, keast)
    zero = jnp.zeros_like(vert_sqrt)
    mix = jnp.concatenate(
        [
            jnp.concatenate([vert_sqrt, vert_sqrt, zero, zero], 1),
            jnp.concatenate([zero, zero, vert_sqrt, vert_sqrt], 1),
        ],
        0,
    )
    part, table = gather(field.reshape(-1, LANES), mix, w_lists, s_lists)
    north = lax.ppermute(jnp.stack([part[0], part[2]]), "lat", down)
    south = lax.ppermute(jnp.stack([part[0], part[1]]), "lat", up)
    out, west_out, east_out = adjoint(
        part, north, south, table, mix, w_lists, s_lists, kext, kwest, keast, rows
    )
    from_east = lax.ppermute(west_out, "lon", westward)
    from_west = lax.ppermute(east_out, "lon", eastward)
    from_east = swap_halves(from_east)
    from_west = swap_halves(from_west)
    return from_tiles(finish(out, from_west, from_east, control2), control.shape)


def swap_halves(x):
    return jnp.concatenate([x[:, :, 64:], x[:, :, :64]], 2)


def solution(mesh):
    in_specs = (
        P(None, "lat", "lon"),
        P(),
        P("lat", "lon"),
        P("lat", "lon"),
        P(("lat", "lon"), None),
        P(("lat", "lon")),
        P(None, ("lat", "lon")),
        P(("lat", "lon")),
        P(("lat", "lon")),
        P(("lat", "lon")),
    )
    out_specs = P(None, "lat", "lon")
    return jax.shard_map(body, mesh=mesh, in_specs=in_specs, out_specs=out_specs, check_vma=False)
```

```python
import functools

import jax
import jax.numpy as jnp
from jax import lax
from jax.experimental import pallas as pl
from jax.experimental.pallas import tpu as pltpu
from jax.sharding import PartitionSpec as P

STEPS = 4
CAP = 16
GROUPS = 8
LANES = 128
VMEM_BYTES = 62 * 1024 * 1024
F32 = jnp.float32
BF16 = jnp.bfloat16
I32 = jnp.int32


def dot(a, b):
    return jnp.dot(a, b, preferred_element_type=F32)


def dot_nt(a, b):
    return lax.dot_general(a, b, (((1,), (1,)), ((), ())), preferred_element_type=F32)


def split(x):
    high = x.astype(BF16)
    return high, (x - high.astype(F32)).astype(BF16)


def iota(shape, axis):
    return lax.broadcasted_iota(I32, shape, axis)


def pack_kernel(n_lon, count_ref, owner_ref, cell_ref, scalar_ref, w_ref, wsend_ref, ssend_ref):
    n_lat = wsend_ref.shape[1]
    devices = n_lat * n_lon
    levels, total = w_ref.shape
    slot_id = iota((1, total), 1)
    live = slot_id < count_ref[0]
    tile = owner_ref[...]
    owner = jnp.where(live, lax.rem(tile, n_lon) * n_lat + lax.div(tile, n_lon), -1)
    cell = cell_ref[...]
    row = cell >> 10
    hot = iota((devices, total), 0) == owner
    classes = (row < STEPS, (row >= STEPS) & (row < 12), row >= 12)
    tables = [(hot & c).astype(F32) for c in classes]
    tri = (iota((total, total), 0) < iota((total, total), 1)).astype(F32).astype(BF16)
    stack = jnp.concatenate(tables, 0)
    earlier = dot(stack.astype(BF16), tri)
    first = jnp.sum(tables[0], axis=1, keepdims=True)
    place = (
        tables[0] * earlier[:devices]
        + tables[1] * (first + earlier[devices : 2 * devices])
        + tables[2] * ((CAP - 1.0) - earlier[2 * devices :])
    )
    slot = jnp.sum(place, axis=0, keepdims=True).astype(I32)
    dest = jnp.where(live, owner * CAP + slot, -1)
    weights = w_ref[...]
    blank = jnp.zeros_like(weights)
    lower = jnp.concatenate([weights, blank], 0)
    upper = jnp.concatenate([blank, weights], 0)
    rows = min(128, devices * 8)
    for chunk in range(devices * 8 // rows):
        r = iota((rows, total), 0) + chunk * rows
        base = (r >> 3) * CAP + (r & 7)
        p0 = (base == dest).astype(F32).astype(BF16)
        p1 = (base + 8 == dest).astype(F32).astype(BF16)
        out = dot_nt(p0, lower) + dot_nt(p1, upper)
        out = out.reshape(rows // 8, 8, LANES).astype(BF16)
        for t in range(rows // 8):
            to = chunk * (rows // 8) + t
            wsend_ref[to // n_lat, to % n_lat] = out[t]
    k = iota((LANES, total), 0)
    kind = k >> 4
    match = (k & 15) == slot
    val = jnp.where(
        kind == 0,
        scalar_ref[0:1, :],
        jnp.where(
            kind == 1,
            scalar_ref[1:2, :],
            jnp.where(kind == 2, (cell >> 7).astype(F32), (cell & 127).astype(F32)),
        ),
    )
    table = jnp.where(match & (kind < 4), val, 0.0).astype(BF16)
    scal = dot_nt(hot.astype(F32).astype(BF16), table)
    ssend_ref[...] = scal.reshape(n_lon, n_lat, 1, LANES)


def pack(count, owner, cell, scalars, weights, n_lat, n_lon):
    vm = pl.BlockSpec(memory_space=pltpu.VMEM)
    return pl.pallas_call(
        functools.partial(pack_kernel, n_lon),
        out_shape=(
            jax.ShapeDtypeStruct((n_lon, n_lat, 8, LANES), BF16),
            jax.ShapeDtypeStruct((n_lon, n_lat, 1, LANES), F32),
        ),
        in_specs=[pl.BlockSpec(memory_space=pltpu.SMEM)] + [vm] * 4,
        out_specs=(vm, vm),
        compiler_params=pltpu.CompilerParams(vmem_limit_bytes=VMEM_BYTES),
        name="pack",
    )(count, owner, cell, scalars, weights)


MESH = pl.DeviceIdType.MESH


def remote(src, dst, send_sem, recv_sem, where):
    return pltpu.make_async_remote_copy(
        src_ref=src, dst_ref=dst, send_sem=send_sem, recv_sem=recv_sem,
        device_id=where, device_id_type=MESH,
    )


def wait_bytes(ref, sem):
    pltpu.make_async_copy(ref, ref, sem).wait()


def tile_rows(i, block):
    return pl.ds((i // 8) * 64 + block * 8 + i % 8, 64, stride=128)


def to_tiles(x):
    levels, rows, cols = x.shape
    x = x.reshape(levels, rows // 8, 8, cols // LANES, LANES).transpose(0, 1, 3, 2, 4)
    return x.reshape(-1, LANES)


def from_tiles(x, shape):
    levels, rows, cols = shape
    x = x.reshape(levels, rows // 8, cols // LANES, 8, LANES).transpose(0, 1, 3, 2, 4)
    return x.reshape(shape)


def turn_in(load, store):
    for p in range(4):
        t = jnp.concatenate([load(p), load(p + 4)], 0).T
        store(2 * p, t[:64])
        store(2 * p + 1, t[64:])


def wrap_low(v, edge):
    rolled = pltpu.roll(v, 1, 0)
    sub = iota(v.shape, 0)
    lane = iota(v.shape, 1)
    return jnp.where(sub == 0, jnp.where(lane < 64, edge, pltpu.roll(rolled, 64, 1)), rolled)


def wrap_high(v, edge):
    rolled = pltpu.roll(v, GROUPS - 1, 0)
    sub = iota(v.shape, 0)
    lane = iota(v.shape, 1)
    return jnp.where(sub == GROUPS - 1, jnp.where(lane >= 64, edge, pltpu.roll(rolled, 64, 1)), rolled)


def turn_coeffs(kx, kt):
    def store(g, t):
        kt[pl.ds(STEPS * 8 + g, 64, stride=8), :] = t

    turn_in(lambda p: kx[:, p * LANES : (p + 1) * LANES], store)


def edge_rows(ref, i, t):
    row = ref[pl.ds(t, 1), :] if i is None else ref[i, pl.ds(t, 1), :]
    return pltpu.roll(jnp.broadcast_to(row, (8, LANES)), 64, 1)


def close_row(field, base, west, east, i):
    for t in range(STEPS):
        v = field[pl.ds(base + (64 + t) * 8, 8), :]
        field[pl.ds(base + t * 8, 8), :] = wrap_low(v, edge_rows(west, i, t))
        v = field[pl.ds(base + (4 + t) * 8, 8), :]
        field[pl.ds(base + (68 + t) * 8, 8), :] = wrap_high(v, edge_rows(east, i, t))


def spread_coeffs(kt, klat, klon):
    both = jnp.concatenate(list(split(kt[...])), 1)
    r = iota((256, 256), 0)
    c = iota((256, 256), 1)
    same = ((r >> 6) & 1) == ((c >> 6) & 1)
    want = (r & 63) - 32 * (c >> 7)

    def one(i, carry):
        pick = (same & (want == i)).astype(F32).astype(BF16)
        out = dot(both, pick)
        klat[i] = out[:, :LANES]
        klon[i] = out[:, LANES:]
        return carry

    lax.fori_loop(0, klat.shape[0], one, 0)


def forward_kernel(n_lat, n_lon, c_ref, kap_ref, w_ref, s_ref, out_ref, kt_ref, wo_ref, so_ref, *scratch):
    s0, s1, kx, klat, klon, w1, s1s, knorth, ksouth, ebuf, wbuf, west, east = scratch[:13]
    kebuf, kwbuf, kwest, keast, bulk, ksem, esem, ksem2, lsem = scratch[13:]
    rows = ebuf.shape[0]
    ext = rows + 2 * STEPS
    wide = 64 + 2 * STEPS
    a, b = lax.axis_index("lat"), lax.axis_index("lon")
    barrier = pltpu.get_barrier_semaphore()

    def lon_peer(step):
        return lax.rem(b + step, n_lon)

    def lat_peer(step):
        return lax.rem(a + step, n_lat)

    for step in range(1, n_lon):
        pl.semaphore_signal(barrier, inc=1, device_id=(a, lon_peer(step)), device_id_type=MESH)
    for step in range(1, n_lat):
        pl.semaphore_signal(barrier, inc=1, device_id=(lat_peer(step), b), device_id_type=MESH)

    @pl.when(a == 0)
    def _():
        knorth[...] = jnp.zeros_like(knorth)

    @pl.when(a == n_lat - 1)
    def _():
        ksouth[...] = jnp.zeros_like(ksouth)

    own1 = (
        pltpu.make_async_copy(w_ref.at[b], w1.at[b], lsem.at[0]),
        pltpu.make_async_copy(s_ref.at[b], s1s.at[b], lsem.at[1]),
    )
    for c in own1:
        c.start()
    pl.semaphore_wait(barrier, n_lon + n_lat - 2)
    southward = remote(kap_ref.at[:, rows // STEPS - 1], knorth, ksem.at[0], ksem.at[1], (lax.rem(a + 1, n_lat), b))
    northward = remote(kap_ref.at[:, 0], ksouth, ksem.at[2], ksem.at[3], (lax.rem(a + n_lat - 1, n_lat), b))

    @pl.when(a < n_lat - 1)
    def _():
        southward.start()

    @pl.when(a > 0)
    def _():
        northward.start()

    for step in range(1, n_lon):
        t = lon_peer(step)
        remote(w_ref.at[t], w1.at[b], bulk.at[0], bulk.at[1], (a, t)).start()
        remote(s_ref.at[t], s1s.at[b], bulk.at[2], bulk.at[3], (a, t)).start()

    def turn(i, carry):
        def store(g, t):
            s0[pl.ds((i * wide + STEPS) * 8 + g, 64, stride=8), :] = t

        turn_in(lambda p: c_ref[tile_rows(i, p), :], store)
        for t in range(STEPS):
            ebuf[i, pl.ds(t, 1), :] = s0[pl.ds((i * wide + 64 + t) * 8 + 7, 1), :]
            wbuf[i, pl.ds(t, 1), :] = s0[pl.ds((i * wide + 4 + t) * 8, 1), :]
        return carry

    lax.fori_loop(0, rows, turn, 0)
    at_east, at_west = (a, lax.rem(b + 1, n_lon)), (a, lax.rem(b + n_lon - 1, n_lon))

    @pl.when(a > 0)
    def _():
        southward.wait_recv()

    @pl.when(a < n_lat - 1)
    def _():
        northward.wait_recv()

    for f in range(2):
        base = 32 * f
        kx[base : base + STEPS, :] = knorth[f]
        for block in range(rows // STEPS):
            kx[base + STEPS + STEPS * block : base + 2 * STEPS + STEPS * block, :] = kap_ref[f, block]
        kx[base + rows + STEPS : base + rows + 2 * STEPS, :] = ksouth[f]
        kx[base + ext : base + 32, :] = jnp.zeros((32 - ext, kx.shape[1]), F32)
    turn_coeffs(kx, kt_ref)
    for t in range(STEPS):
        kebuf[pl.ds(t, 1), :] = kt_ref[pl.ds((64 + t) * 8 + 7, 1), :]
        kwbuf[pl.ds(t, 1), :] = kt_ref[pl.ds((4 + t) * 8, 1), :]
    edges = (
        remote(ebuf, west, esem.at[0], esem.at[1], at_east),
        remote(wbuf, east, esem.at[2], esem.at[3], at_west),
        remote(kebuf, kwest, ksem2.at[0], ksem2.at[1], at_east),
        remote(kwbuf, keast, ksem2.at[2], ksem2.at[3], at_west),
    )
    for c in edges:
        c.start()

    for c in own1:
        c.wait()
    for ref, src, at in ((w1, w_ref, 0), (s1s, s_ref, 2)):
        part = pl.ds(0, n_lon - 1)
        wait_bytes(src.at[part], bulk.at[at])
        wait_bytes(ref.at[part], bulk.at[at + 1])

    def lists(t):
        return (t, jnp.maximum(t - 1, 0), jnp.minimum(t + 1, n_lat - 1))

    for step in range(1, n_lat):
        t = lat_peer(step)
        for n, of in enumerate(lists(t)):
            remote(w1.at[:, of], wo_ref.at[n, a], bulk.at[4], bulk.at[5], (t, b)).start()
            remote(s1s.at[:, of], so_ref.at[n, a], bulk.at[6], bulk.at[7], (t, b)).start()
    own2 = []
    for n, of in enumerate(lists(a)):
        own2.append(pltpu.make_async_copy(w1.at[:, of], wo_ref.at[n, a], lsem.at[2 + 2 * n]))
        own2.append(pltpu.make_async_copy(s1s.at[:, of], so_ref.at[n, a], lsem.at[3 + 2 * n]))
    for c in own2:
        c.start()

    for c in edges:
        c.wait()
    close_row(kt_ref, 0, kwest, keast, None)

    def close(i, carry):
        close_row(s0, pl.multiple_of(i * wide * 8, 8), west, east, i)
        return carry

    lax.fori_loop(0, rows, close, 0)
    spread_coeffs(kt_ref, klat, klon)

    def lat(q, carry):
        at = pl.ds(pl.multiple_of(q * 8, 8), 8)
        x = {STEPS + i: s0[pl.ds(pl.multiple_of((i * wide + q) * 8, 8), 8), :] for i in range(rows)}
        k = [klat[i, at, :] for i in range(ext)]
        for step in range(STEPS):
            lo, hi = min(x), max(x)
            d = {}
            for i in range(lo - 1, hi + 1):
                if i < lo:
                    d[i] = x[lo]
                elif i == hi:
                    d[i] = -x[hi]
                else:
                    d[i] = x[i + 1] - x[i]
            new = {}
            for i in range(lo - 1, hi + 2):
                if i < lo:
                    new[i] = k[i] * x[lo]
                elif i > hi:
                    new[i] = k[i] * x[hi]
                else:
                    new[i] = x[i] + k[i] * (d[i] - d[i - 1])
            x = new
        for i in range(ext):
            s1[i, at, :] = x[i]
        return carry

    lax.fori_loop(0, wide, lat, 0)

    def lon(i, carry):
        stages = [[] for _ in range(STEPS + 1)]
        diffs = [[] for _ in range(STEPS)]
        coef = []
        for q in range(wide):
            stages[0].append(s1[i, q * 8 : q * 8 + 8, :])
            coef.append(klon[i, q * 8 : q * 8 + 8, :])
            for s in range(STEPS):
                x = stages[s]
                n = len(x)
                if n >= 2:
                    diffs[s].append(x[n - 1] - x[n - 2])
                if n >= 3:
                    mid = n - 2
                    stages[s + 1].append(x[mid] + coef[mid + s] * (diffs[s][-1] - diffs[s][-2]))
                    if s == STEPS - 1:
                        out_ref[i, mid - 1] = stages[STEPS][-1]
        return carry

    lax.fori_loop(0, ext, lon, 0)
    for c in own2:
        c.wait()

    @pl.when(a < n_lat - 1)
    def _():
        southward.wait_send()

    @pl.when(a > 0)
    def _():
        northward.wait_send()

    for ref, at in ((wo_ref, 4), (so_ref, 6)):
        part = ref.at[:, pl.ds(0, n_lat - 1)]
        wait_bytes(part, bulk.at[at])
        wait_bytes(part, bulk.at[at + 1])


def forward(control2, kap, wsend, ssend, n_lat, n_lon):
    rows = kap.shape[1] * kap.shape[2]
    ext = rows + 2 * STEPS
    wide = 64 + 2 * STEPS
    vm = pl.BlockSpec(memory_space=pltpu.VMEM)
    edge = pltpu.VMEM((rows, STEPS, LANES), F32)
    kedge = pltpu.VMEM((STEPS, LANES), F32)
    krows = pltpu.VMEM((2, STEPS, kap.shape[3]), F32)
    dma = pltpu.SemaphoreType.DMA
    return pl.pallas_call(
        functools.partial(forward_kernel, n_lat, n_lon),
        out_shape=(
            jax.ShapeDtypeStruct((ext, 64, 8, LANES), F32),
            jax.ShapeDtypeStruct((wide * 8, LANES), F32),
            jax.ShapeDtypeStruct((3, n_lat, n_lon, 8, LANES), BF16),
            jax.ShapeDtypeStruct((3, n_lat, n_lon, 1, LANES), F32),
        ),
        in_specs=[vm] * 4,
        out_specs=(vm,) * 4,
        scratch_shapes=[
            pltpu.VMEM((rows * wide * 8, LANES), F32),
            pltpu.VMEM((ext, wide * 8, LANES), F32),
            pltpu.VMEM((64, kap.shape[3]), F32),
            pltpu.VMEM((ext, wide * 8, LANES), F32),
            pltpu.VMEM((ext, wide * 8, LANES), F32),
            pltpu.VMEM((n_lon, n_lat, 8, LANES), BF16),
            pltpu.VMEM((n_lon, n_lat, 1, LANES), F32),
            krows, krows, edge, edge, edge, edge, kedge, kedge, kedge, kedge,
            dma((8,)), dma((4,)), dma((4,)), dma((4,)), dma((8,)),
        ],
        compiler_params=pltpu.CompilerParams(
            vmem_limit_bytes=VMEM_BYTES, collective_id=0, has_side_effects=True),
        name="route_forward",
    )(control2, kap, wsend, ssend)


def swap_kernel(n_lat, part_ref, north_ref, south_ref, sem):
    a, b = lax.axis_index("lat"), lax.axis_index("lon")
    up, down = lax.rem(a + n_lat - 1, n_lat), lax.rem(a + 1, n_lat)
    barrier = pltpu.get_barrier_semaphore()
    for t in (up, down):
        pl.semaphore_signal(barrier, inc=1, device_id=(t, b), device_id_type=MESH)
    pl.semaphore_wait(barrier, 2)
    copies = [
        remote(part_ref.at[pl.ds(0, 2)], south_ref, sem.at[0], sem.at[1], (up, b)),
        remote(part_ref.at[pl.ds(2, 2)], north_ref, sem.at[2], sem.at[3], (down, b)),
    ]
    for c in copies:
        c.start()
    for c in copies:
        c.wait()


def swap(part, n_lat):
    vm = pl.BlockSpec(memory_space=pltpu.VMEM)
    shape = jax.ShapeDtypeStruct((2,) + part.shape[1:], F32)
    return pl.pallas_call(
        functools.partial(swap_kernel, n_lat),
        out_shape=(shape, shape),
        in_specs=[vm],
        out_specs=(vm, vm),
        scratch_shapes=[pltpu.SemaphoreType.DMA((4,))],
        compiler_params=pltpu.CompilerParams(collective_id=1, has_side_effects=True),
        name="swap",
    )(part)


def rims_kernel(n_lon, west_ref, east_ref, from_west_ref, from_east_ref, sem):
    a, b = lax.axis_index("lat"), lax.axis_index("lon")
    left, right = lax.rem(b + n_lon - 1, n_lon), lax.rem(b + 1, n_lon)
    barrier = pltpu.get_barrier_semaphore()
    for t in (left, right):
        pl.semaphore_signal(barrier, inc=1, device_id=(a, t), device_id_type=MESH)
    pl.semaphore_wait(barrier, 2)
    copies = [
        remote(west_ref, from_east_ref, sem.at[0], sem.at[1], (a, left)),
        remote(east_ref, from_west_ref, sem.at[2], sem.at[3], (a, right)),
    ]
    for c in copies:
        c.start()
    for c in copies:
        c.wait()


def rims(west, east, n_lon):
    vm = pl.BlockSpec(memory_space=pltpu.VMEM)
    shape = jax.ShapeDtypeStruct(west.shape, F32)
    return pl.pallas_call(
        functools.partial(rims_kernel, n_lon),
        out_shape=(shape, shape),
        in_specs=[vm, vm],
        out_specs=(vm, vm),
        scratch_shapes=[pltpu.SemaphoreType.DMA((4,))],
        compiler_params=pltpu.CompilerParams(collective_id=2, has_side_effects=True),
        name="rims",
    )(west, east)


def mix_table(vert):
    twice = jnp.concatenate([vert, vert], 1)
    none = jnp.zeros_like(twice)
    return jnp.concatenate([jnp.concatenate([twice, none], 1), jnp.concatenate([none, twice], 1)], 0)


def level_mix(w_ref, n, mix_ref, u):
    w = w_ref[n]
    w = w.astype(F32).reshape(-1, LANES).astype(BF16)
    high, low = split(mix_table(mix_ref[...]))
    both = dot(jnp.concatenate([w, w], 1), jnp.concatenate([high, low], 0))
    u[0] = both[:, :LANES]
    u[1] = both[:, LANES:]


def list_fields(s_ref, n, have):
    value = s_ref[n].reshape(-1, LANES)
    rinv = pltpu.roll(value, LANES - 16, 1)
    cell = (pltpu.roll(value, LANES - 32, 1) * 128.0 + pltpu.roll(value, LANES - 48, 1)).astype(I32)
    row = cell >> 10
    col = cell & 1023
    where = (col & 63) * 8 + ((col >> 6) & 7)
    valid = (rinv > 0.5) & (iota(value.shape, 1) < jnp.where(have[n] > 0, CAP, 0))
    return value, rinv, row, where, col >> 9, valid


def count_max(mask, weight):
    return jnp.max(jnp.where(mask, weight, 0), axis=1, keepdims=True)


def relevant(row, valid):
    return (valid, valid & (row >= 12), valid & (row < STEPS))


def tables(number, row, where, valid):
    lane = iota(row.shape, 1)
    front = valid & (row < 12)
    back = valid & (row >= 12)
    slot = lane + 1
    depth = CAP - lane
    need = relevant(row, valid)[number]
    shift = (STEPS, -12, 20)[number]
    gather = jnp.where(need, (row + shift) * 512 + where, 0)
    if number == 0:
        first = jnp.where(front, row * 512 + where, 12 * 512)
        second = jnp.where(back, (row - 12) * 512 + where, 4 * 512)
        nf = count_max(front, slot)
        nb = count_max(back, depth)
        mid = jnp.maximum(nf, nb - 4)
        late = jnp.maximum(nf - 4, nb)
        n0, n1, n2, n3 = mid, late, nf, nb
    elif number == 1:
        first = jnp.where(need, (row - 12) * 512 + where, 4 * 512)
        second = first
        n0 = n1 = n2 = n3 = count_max(need, depth)
    else:
        first = jnp.where(need, row * 512 + where, 4 * 512)
        second = first
        n0 = n1 = n2 = n3 = count_max(need, slot)
    out = jnp.where(lane < 16, gather, 0)
    out = jnp.where((lane >= 16) & (lane < 32), pltpu.roll(first, 16, 1), out)
    out = jnp.where((lane >= 32) & (lane < 48), pltpu.roll(second, 32, 1), out)
    for at, n in ((48, n0), (49, n1), (50, n2), (51, n3)):
        out = jnp.where(lane == at, n, out)
    return out


def gather_kernel(have_ref, field_ref, mix_ref, w_ref, s_ref, part_ref, table_ref, u, picked, smem, sem):
    devices = table_ref.shape[1]
    info = []
    for n in range(3):
        value, rinv, row, where, gh, valid = list_fields(s_ref, n, have_ref)
        table_ref[n] = tables(n, row, where, valid)
        info.append((gh, relevant(row, valid)[n]))
    copy = pltpu.make_async_copy(table_ref, smem, sem)
    copy.start()
    for n in range(3):
        level_mix(w_ref, n, mix_ref, u.at[n])
    copy.wait()

    def fetch(n, s, slots):
        for k in slots:
            r = smem[n, s, k]
            picked[n, k, pl.ds(s, 1), :] = field_ref[pl.ds(r, 1), :]

    def source(s, carry):
        fetch(0, s, (0, 1, 2, 3, 12, 13, 14, 15))
        fetch(1, s, (12, 13, 14, 15))
        fetch(2, s, (0, 1, 2, 3))
        mid, late = smem[0, s, 48], smem[0, s, 49]
        north, south = smem[1, s, 48], smem[2, s, 48]

        @pl.when(mid > 4)
        def _():
            fetch(0, s, (4, 5, 6, 7))

        @pl.when(late > 4)
        def _():
            fetch(0, s, (8, 9, 10, 11))

        @pl.when(north > 4)
        def _():
            fetch(1, s, range(12))

        @pl.when(south > 4)
        def _():
            fetch(2, s, range(4, 16))

        return carry

    lax.fori_loop(0, devices, source, 0)
    lane = iota((devices, LANES), 1)
    for n in range(3):
        gh, keep = info[n]
        gh = jnp.where(keep, gh, -1)
        total = jnp.zeros((devices, LANES), F32)
        for k in range(CAP):
            uk = u[n, k // 8, pl.ds(k % 8, devices, stride=8), :]
            sel = jnp.broadcast_to(gh[:, k : k + 1], uk.shape) == (lane >> 6)
            prod = jnp.where(sel, uk * picked[n, k], 0.0)
            total = jnp.where(lane == k, jnp.sum(prod, axis=1, keepdims=True), total)
        total = total.T[:CAP]
        for at in ((0, 2), (1,), (3,))[n]:
            part_ref[at] = total


def gather(have, field, mix, wo, so):
    devices = wo.shape[1] * wo.shape[2]
    vm = pl.BlockSpec(memory_space=pltpu.VMEM)
    return pl.pallas_call(
        gather_kernel,
        out_shape=(
            jax.ShapeDtypeStruct((4, CAP, devices), F32),
            jax.ShapeDtypeStruct((3, devices, LANES), I32),
        ),
        in_specs=[pl.BlockSpec(memory_space=pltpu.SMEM)] + [vm] * 4,
        out_specs=(vm, vm),
        scratch_shapes=[
            pltpu.VMEM((3, 2, devices * 8, LANES), F32),
            pltpu.VMEM((3, CAP, devices, LANES), F32),
            pltpu.SMEM((3, devices, LANES), I32),
            pltpu.SemaphoreType.DMA,
        ],
        compiler_params=pltpu.CompilerParams(vmem_limit_bytes=VMEM_BYTES),
        name="gather",
    )(have, field, mix, wo, so)


def adjoint_kernel(have_ref, part_ref, north_ref, south_ref, table_ref, mix_ref, w_ref, s_ref, kt_ref, *refs):
    out_ref, west_ref, east_ref, u, force, a_north, a_front, a_back, a_south, s1, klat, klon = refs
    devices = part_ref.shape[2]
    rows = out_ref.shape[0]
    ext = rows + 2 * STEPS
    wide = 64 + 2 * STEPS
    for a in (a_north, a_front, a_back, a_south):
        size = a.shape[0] // 64

        def clear(i, carry, a=a):
            a[pl.ds(pl.multiple_of(i * 64, 64), 64), :] = jnp.zeros((64, LANES), F32)
            return carry

        lax.fori_loop(0, size, clear, 0)
    spread_coeffs(kt_ref, klat, klon)
    lane = iota((devices, LANES), 1)
    north = [jnp.where(have_ref[1] > 0, north_ref[n], 0.0) for n in range(2)]
    south = [jnp.where(have_ref[2] > 0, south_ref[n], 0.0) for n in range(2)]
    totals = (part_ref[0] + north[1] + south[1], part_ref[1] + north[0], part_ref[3] + south[0])
    blank = jnp.zeros((LANES - CAP, devices), F32)
    totals = [jnp.concatenate([t, blank], 0).T for t in totals]
    for n in range(3):
        level_mix(w_ref, n, mix_ref, u)
        value, rinv, row, where, gh, valid = list_fields(s_ref, n, have_ref)
        misfit = rinv * (totals[n] - value)
        for k in range(CAP):
            uk = u[k // 8, pl.ds(k % 8, devices, stride=8), :]
            sel = jnp.broadcast_to(gh[:, k : k + 1], uk.shape) == (lane >> 6)
            force[n, k] = jnp.where(sel, uk * misfit[:, k : k + 1], 0.0)

    def add(a, n, s, k, at):
        r = table_ref[n, s, at + k]
        a[pl.ds(r, 1), :] += force[n, k, pl.ds(s, 1), :]

    def source(s, carry):
        for k in range(4):
            add(a_front, 0, s, k, 16)
            add(a_back, 0, s, CAP - 1 - k, 32)
            add(a_north, 1, s, CAP - 1 - k, 16)
            add(a_south, 2, s, k, 16)
        nf, nb = table_ref[0, s, 50], table_ref[0, s, 51]
        north, south = table_ref[1, s, 48], table_ref[2, s, 48]
        for g in range(1, 4):
            @pl.when(nf > 4 * g)
            def _(g=g):
                for k in range(4 * g, 4 * g + 4):
                    add(a_front, 0, s, k, 16)

        @pl.when(jnp.maximum(nb, jnp.maximum(north, south)) > 4)
        def _():
            for k in range(4, CAP):
                add(a_back, 0, s, CAP - 1 - k, 32)
                add(a_north, 1, s, CAP - 1 - k, 16)
                add(a_south, 2, s, k, 16)

        return carry

    lax.fori_loop(0, devices, source, 0)

    def lon(source, first, count):
        def one(i, carry):
            stages = [{} for _ in range(STEPS + 1)]
            k = {}
            h = [{} for _ in range(STEPS)]
            d = [{} for _ in range(STEPS)]

            def coef(q):
                if q not in k:
                    k[q] = klon[first + i, (q + STEPS) * 8 : (q + STEPS) * 8 + 8, :]
                return k[q]

            for q in range(-1, 64 + 2 * STEPS + 1):
                for s in range(STEPS):
                    lo, hi = -s, 63 + s
                    at = q - s
                    if s == 0 and lo <= at <= hi:
                        stages[0][at] = source[pl.ds(pl.multiple_of((i * 64 + at) * 8, 8), 8), :]
                    if lo <= at <= hi + 2:
                        if at == lo:
                            h[s][at] = coef(at) * stages[s][at]
                            d[s][at - 1] = h[s][at]
                            stages[s + 1][at - 1] = h[s][at]
                        else:
                            if at <= hi:
                                h[s][at] = coef(at) * stages[s][at]
                            if at <= hi:
                                d[s][at - 1] = h[s][at] - h[s][at - 1]
                            elif at == hi + 1:
                                d[s][at - 1] = -h[s][at - 1]
                            m = at - 1
                            if m <= hi:
                                stages[s + 1][m] = stages[s][m] + (d[s][m] - d[s][m - 1])
                            else:
                                stages[s + 1][m] = -d[s][m - 1]
            for q in range(-STEPS, 64 + STEPS):
                s1[first + i, (q + STEPS) * 8 : (q + STEPS) * 8 + 8, :] = stages[STEPS][q]
            return carry

        lax.fori_loop(0, count, one, 0)

    lon(a_north, 0, STEPS)
    lon(a_front, STEPS, 12)
    lon(a_back, rows, STEPS)
    lon(a_south, rows + STEPS, STEPS)

    def lat(q, carry):
        at = pl.ds(pl.multiple_of(q * 8, 8), 8)
        x = {i: s1[i, at, :] for i in range(ext)}
        k = [klat[i, at, :] for i in range(ext)]
        for step in range(STEPS):
            h = {i: k[i] * x[i] for i in x}
            lo, hi = min(x), max(x)
            d = {i: h[i + 1] - h[i] for i in range(lo, hi)}
            x = {i: x[i] + (d[i] - d[i - 1]) for i in range(lo + 1, hi)}
        for i in range(rows):
            s1[i, at, :] = x[STEPS + i]
        return carry

    lax.fori_loop(0, wide, lat, 0)

    def fold(i, carry):
        zero = jnp.zeros((8, LANES), F32)

        def body(q, carry):
            out_ref[i, q] = s1[i, pl.ds(pl.multiple_of((q + STEPS) * 8, 8), 8), :]
            return carry

        lax.fori_loop(STEPS, 64 - STEPS, body, 0, unroll=8)
        for t in range(STEPS):
            low = s1[i, t * 8 : t * 8 + 8, :]
            high = s1[i, (68 + t) * 8 : (68 + t) * 8 + 8, :]
            west_ref[i, pl.ds(t, 1), :] = low[0:1]
            east_ref[i, pl.ds(t, 1), :] = high[GROUPS - 1 :]
            out_ref[i, 60 + t] = s1[i, (64 + t) * 8 : (64 + t) * 8 + 8, :] + wrap_high(low, zero)
            out_ref[i, t] = s1[i, (4 + t) * 8 : (4 + t) * 8 + 8, :] + wrap_low(high, zero)
        return carry

    lax.fori_loop(0, rows, fold, 0)


def adjoint(have, part, north, south, table, mix, wo, so, kt, rows):
    devices = part.shape[2]
    ext = rows + 2 * STEPS
    wide = 64 + 2 * STEPS
    vm = pl.BlockSpec(memory_space=pltpu.VMEM)
    sm = pl.BlockSpec(memory_space=pltpu.SMEM)
    edge = jax.ShapeDtypeStruct((rows, STEPS, LANES), F32)
    return pl.pallas_call(
        adjoint_kernel,
        out_shape=(jax.ShapeDtypeStruct((rows, 64, 8, LANES), F32), edge, edge),
        in_specs=[sm] + [vm] * 3 + [sm] + [vm] * 4,
        out_specs=(vm, vm, vm),
        scratch_shapes=[
            pltpu.VMEM((2, devices * 8, LANES), F32),
            pltpu.VMEM((3, CAP, devices, LANES), F32),
            pltpu.VMEM((4 * 512 + 64, LANES), F32),
            pltpu.VMEM((12 * 512 + 64, LANES), F32),
            pltpu.VMEM((4 * 512 + 64, LANES), F32),
            pltpu.VMEM((4 * 512 + 64, LANES), F32),
            pltpu.VMEM((ext, wide * 8, LANES), F32),
            pltpu.VMEM((ext, wide * 8, LANES), F32),
            pltpu.VMEM((ext, wide * 8, LANES), F32),
        ],
        compiler_params=pltpu.CompilerParams(vmem_limit_bytes=VMEM_BYTES),
        name="adjoint_filter",
    )(have, part, north, south, table, mix, wo, so, kt)


def finish_kernel(field_ref, west_ref, east_ref, c_ref, out_ref, s0):
    rows = west_ref.shape[0]
    lane = iota((1, LANES), 1)

    def turn(i, carry):
        def copy(q, c):
            s0[pl.ds(pl.multiple_of(q * 8, 8), 8), :] = field_ref[i, q]
            return c

        lax.fori_loop(0, 64, copy, 0, unroll=8)
        for t in range(STEPS):
            row = t * 8
            s0[row : row + 1, :] += jnp.where(lane < 64, pltpu.roll(west_ref[i, pl.ds(t, 1), :], 64, 1), 0.0)
            row = (60 + t) * 8 + GROUPS - 1
            s0[row : row + 1, :] += jnp.where(lane >= 64, pltpu.roll(east_ref[i, pl.ds(t, 1), :], 64, 1), 0.0)
        for p in range(4):
            t = jnp.concatenate(
                [s0[pl.ds(2 * p, 64, stride=8), :], s0[pl.ds(2 * p + 1, 64, stride=8), :]], 0
            ).T
            for gh in range(2):
                at = tile_rows(i, 4 * gh + p)
                out_ref[at, :] = c_ref[at, :] + t[gh * 64 : gh * 64 + 64]
        return carry

    lax.fori_loop(0, rows, turn, 0)


def finish(field, west, east, control2):
    vm = pl.BlockSpec(memory_space=pltpu.VMEM)
    return pl.pallas_call(
        finish_kernel,
        out_shape=jax.ShapeDtypeStruct(control2.shape, F32),
        in_specs=[vm] * 4,
        out_specs=vm,
        scratch_shapes=[pltpu.VMEM((64 * 8, LANES), F32)],
        compiler_params=pltpu.CompilerParams(vmem_limit_bytes=VMEM_BYTES),
        name="finish",
    )(field, west, east, control2)


def body(control, vert_sqrt, kappa_lat, kappa_lon, obs_owner, obs_cell, obs_weights, obs_value, obs_rinv, obs_count):
    levels, rows, cols = control.shape
    n_lat, n_lon = lax.axis_size("lat"), lax.axis_size("lon")
    total = obs_cell.shape[0]
    a = lax.axis_index("lat")
    have = jnp.stack([jnp.int32(1), (a > 0).astype(I32), (a < n_lat - 1).astype(I32)])
    scalars = jnp.stack([obs_value.astype(F32), obs_rinv.astype(F32)])
    wsend, ssend = pack(
        obs_count, obs_owner.reshape(1, total), obs_cell.reshape(1, total), scalars, obs_weights, n_lat, n_lon
    )
    kap = jnp.stack([kappa_lat, kappa_lon]).reshape(2, rows // STEPS, STEPS, cols)
    control2 = to_tiles(control)
    field, kt, wo, so = forward(control2, kap, wsend, ssend, n_lat, n_lon)
    part, table = gather(have, field.reshape(-1, LANES), vert_sqrt, wo, so)
    north, south = swap(part, n_lat)
    out, west_out, east_out = adjoint(have, part, north, south, table, vert_sqrt, wo, so, kt, rows)
    from_west, from_east = rims(west_out, east_out, n_lon)
    return from_tiles(finish(out, from_west, from_east, control2), control.shape)


def solution(mesh):
    in_specs = (
        P(None, "lat", "lon"),
        P(),
        P("lat", "lon"),
        P("lat", "lon"),
        P(("lat", "lon"), None),
        P(("lat", "lon")),
        P(None, ("lat", "lon")),
        P(("lat", "lon")),
        P(("lat", "lon")),
        P(("lat", "lon")),
    )
    out_specs = P(None, "lat", "lon")
    return jax.shard_map(body, mesh=mesh, in_specs=in_specs, out_specs=out_specs, check_vma=False)
```

```python
import functools

import jax
import jax.numpy as jnp
from jax import lax
from jax.experimental import pallas as pl
from jax.experimental.pallas import tpu as pltpu
from jax.sharding import PartitionSpec as P

STEPS = 4
CAP = 16
GROUPS = 8
LANES = 128
VMEM_BYTES = 62 * 1024 * 1024
F32 = jnp.float32
BF16 = jnp.bfloat16
I32 = jnp.int32


def dot(a, b):
    return jnp.dot(a, b, preferred_element_type=F32)


def dot_nt(a, b):
    return lax.dot_general(a, b, (((1,), (1,)), ((), ())), preferred_element_type=F32)


def split(x):
    high = x.astype(BF16)
    return high, (x - high.astype(F32)).astype(BF16)


def iota(shape, axis):
    return lax.broadcasted_iota(I32, shape, axis)


def pack_kernel(n_lon, count_ref, owner_ref, cell_ref, value_ref, rinv_ref, w_ref, wsend_ref, ssend_ref):
    n_lat = wsend_ref.shape[1]
    devices = n_lat * n_lon
    levels, total = w_ref.shape
    slot_id = iota((1, total), 1)
    live = slot_id < count_ref[0]
    tile = owner_ref[...]
    owner = jnp.where(live, lax.rem(tile, n_lon) * n_lat + lax.div(tile, n_lon), -1)
    cell = cell_ref[...]
    row = cell >> 10
    hot = iota((devices, total), 0) == owner
    classes = (row < STEPS, (row >= STEPS) & (row < 12), row >= 12)
    tables = [(hot & c).astype(F32) for c in classes]
    tri = (iota((total, total), 0) < iota((total, total), 1)).astype(F32).astype(BF16)
    stack = jnp.concatenate(tables, 0)
    earlier = dot(stack.astype(BF16), tri)
    first = jnp.sum(tables[0], axis=1, keepdims=True)
    place = (
        tables[0] * earlier[:devices]
        + tables[1] * (first + earlier[devices : 2 * devices])
        + tables[2] * ((CAP - 1.0) - earlier[2 * devices :])
    )
    slot = jnp.sum(place, axis=0, keepdims=True).astype(I32)
    dest = jnp.where(live, owner * CAP + slot, -1)
    weights = w_ref[...]
    blank = jnp.zeros_like(weights)
    lower = jnp.concatenate([weights, blank], 0)
    upper = jnp.concatenate([blank, weights], 0)
    rows = min(128, devices * 8)
    for chunk in range(devices * 8 // rows):
        r = iota((rows, total), 0) + chunk * rows
        base = (r >> 3) * CAP + (r & 7)
        p0 = (base == dest).astype(F32).astype(BF16)
        p1 = (base + 8 == dest).astype(F32).astype(BF16)
        out = dot_nt(p0, lower) + dot_nt(p1, upper)
        out = out.reshape(rows // 8, 8, LANES).astype(BF16)
        for t in range(rows // 8):
            to = chunk * (rows // 8) + t
            wsend_ref[to // n_lat, to % n_lat] = out[t]
    k = iota((LANES, total), 0)
    kind = k >> 4
    match = (k & 15) == slot
    val = jnp.where(
        kind == 0,
        value_ref[...].astype(F32).reshape(1, total),
        jnp.where(
            kind == 1,
            rinv_ref[...].astype(F32).reshape(1, total),
            jnp.where(kind == 2, (cell >> 7).astype(F32), (cell & 127).astype(F32)),
        ),
    )
    table = jnp.where(match & (kind < 4), val, 0.0).astype(BF16)
    scal = dot_nt(hot.astype(F32).astype(BF16), table)
    ssend_ref[...] = scal.reshape(n_lon, n_lat, 1, LANES)


def pack(count, owner, cell, value, rinv, weights, n_lat, n_lon):
    vm = pl.BlockSpec(memory_space=pltpu.VMEM)
    return pl.pallas_call(
        functools.partial(pack_kernel, n_lon),
        out_shape=(
            jax.ShapeDtypeStruct((n_lon, n_lat, 8, LANES), BF16),
            jax.ShapeDtypeStruct((n_lon, n_lat, 1, LANES), F32),
        ),
        in_specs=[pl.BlockSpec(memory_space=pltpu.SMEM)] + [vm] * 5,
        out_specs=(vm, vm),
        compiler_params=pltpu.CompilerParams(vmem_limit_bytes=VMEM_BYTES),
        name="pack",
    )(count, owner, cell, value, rinv, weights)


MESH = pl.DeviceIdType.MESH


def remote(src, dst, send_sem, recv_sem, where):
    return pltpu.make_async_remote_copy(
        src_ref=src, dst_ref=dst, send_sem=send_sem, recv_sem=recv_sem,
        device_id=where, device_id_type=MESH,
    )


def wait_bytes(ref, sem):
    pltpu.make_async_copy(ref, ref, sem).wait()


def tile_rows(i, block):
    return pl.ds((i // 8) * 4096 + block * 512 + i % 8, 64, stride=8)


def to_tiles(x):
    levels, rows, cols = x.shape
    x = x.reshape(levels, rows // 8, 8, cols // LANES, LANES).transpose(0, 1, 3, 2, 4)
    return x.reshape(levels, -1, 8, LANES)


def from_tiles(x, shape):
    levels, rows, cols = shape
    x = x.reshape(levels, rows // 8, cols // LANES, 8, LANES).transpose(0, 1, 3, 2, 4)
    return x.reshape(shape)


def block_copies(src, dst, sem):
    return [pltpu.make_async_copy(src.at[:, b], dst.at[b], sem) for b in range(dst.shape[0])]


def turn_in(load, store):
    for p in range(4):
        t = jnp.concatenate([load(p), load(p + 4)], 0).T
        store(2 * p, t[:64])
        store(2 * p + 1, t[64:])


def wrap_low(v, edge):
    rolled = pltpu.roll(v, 1, 0)
    sub = iota(v.shape, 0)
    lane = iota(v.shape, 1)
    return jnp.where(sub == 0, jnp.where(lane < 64, edge, pltpu.roll(rolled, 64, 1)), rolled)


def wrap_high(v, edge):
    rolled = pltpu.roll(v, GROUPS - 1, 0)
    sub = iota(v.shape, 0)
    lane = iota(v.shape, 1)
    return jnp.where(sub == GROUPS - 1, jnp.where(lane >= 64, edge, pltpu.roll(rolled, 64, 1)), rolled)


def turn_coeffs(kx, kt):
    def store(g, t):
        kt[pl.ds(STEPS * 8 + g, 64, stride=8), :] = t

    turn_in(lambda p: kx[:, p * LANES : (p + 1) * LANES], store)


def edge_rows(ref, i, t):
    row = ref[pl.ds(t, 1), :] if i is None else ref[i, pl.ds(t, 1), :]
    return pltpu.roll(jnp.broadcast_to(row, (8, LANES)), 64, 1)


def close_row(field, base, west, east, i):
    for t in range(STEPS):
        v = field[pl.ds(base + (64 + t) * 8, 8), :]
        field[pl.ds(base + t * 8, 8), :] = wrap_low(v, edge_rows(west, i, t))
        v = field[pl.ds(base + (4 + t) * 8, 8), :]
        field[pl.ds(base + (68 + t) * 8, 8), :] = wrap_high(v, edge_rows(east, i, t))


def spread_coeffs(kt, klat, klon):
    both = jnp.concatenate(list(split(kt[...])), 1)
    r = iota((256, 256), 0)
    c = iota((256, 256), 1)
    same = ((r >> 6) & 1) == ((c >> 6) & 1)
    want = (r & 63) - 32 * (c >> 7)

    def one(i, carry):
        pick = (same & (want == i)).astype(F32).astype(BF16)
        out = dot(both, pick)
        klat[i] = out[:, :LANES]
        klon[i] = out[:, LANES:]
        return carry

    lax.fori_loop(0, klat.shape[0], one, 0)


def forward_kernel(n_lat, n_lon, c_hbm, kl_ref, kn_ref, w_ref, s_ref, out_hbm, klat_hbm, klon_hbm, wo_ref, so_ref, *scratch):
    s0, s1, kx, klat, klon, w1, s1s, knorth, ksouth, ebuf, wbuf, west, east = scratch[:13]
    kebuf, kwbuf, kwest, keast, bulk, ksem, esem, ksem2, lsem, cv, field, kt_ref, ksend = scratch[13:]
    c_ref = cv.reshape(cv.shape[0] * cv.shape[1] * 8, LANES)
    loads = block_copies(c_hbm, cv, lsem.at[8])
    for c in loads:
        c.start()
    rows = ebuf.shape[0]
    ext = rows + 2 * STEPS
    wide = 64 + 2 * STEPS
    a, b = lax.axis_index("lat"), lax.axis_index("lon")
    barrier = pltpu.get_barrier_semaphore()

    def lon_peer(step):
        return lax.rem(b + step, n_lon)

    def lat_peer(step):
        return lax.rem(a + step, n_lat)

    for step in range(1, n_lon):
        pl.semaphore_signal(barrier, inc=1, device_id=(a, lon_peer(step)), device_id_type=MESH)
    for step in range(1, n_lat):
        pl.semaphore_signal(barrier, inc=1, device_id=(lat_peer(step), b), device_id_type=MESH)

    for f, k_ref in enumerate((kl_ref, kn_ref)):
        ksend[0, f] = k_ref[k_ref.shape[0] - STEPS :, :]
        ksend[1, f] = k_ref[:STEPS, :]

    @pl.when(a == 0)
    def _():
        knorth[...] = jnp.zeros_like(knorth)

    @pl.when(a == n_lat - 1)
    def _():
        ksouth[...] = jnp.zeros_like(ksouth)

    own1 = (
        pltpu.make_async_copy(w_ref.at[b], w1.at[b], lsem.at[0]),
        pltpu.make_async_copy(s_ref.at[b], s1s.at[b], lsem.at[1]),
    )
    for c in own1:
        c.start()
    pl.semaphore_wait(barrier, n_lon + n_lat - 2)
    southward = remote(ksend.at[0], knorth, ksem.at[0], ksem.at[1], (lax.rem(a + 1, n_lat), b))
    northward = remote(ksend.at[1], ksouth, ksem.at[2], ksem.at[3], (lax.rem(a + n_lat - 1, n_lat), b))

    @pl.when(a < n_lat - 1)
    def _():
        southward.start()

    @pl.when(a > 0)
    def _():
        northward.start()

    for step in range(1, n_lon):
        t = lon_peer(step)
        remote(w_ref.at[t], w1.at[b], bulk.at[0], bulk.at[1], (a, t)).start()
        remote(s_ref.at[t], s1s.at[b], bulk.at[2], bulk.at[3], (a, t)).start()

    def turn(i, carry):
        def store(g, t):
            s0[pl.ds((i * wide + STEPS) * 8 + g, 64, stride=8), :] = t

        turn_in(lambda p: c_ref[tile_rows(i, p), :], store)
        for t in range(STEPS):
            ebuf[i, pl.ds(t, 1), :] = s0[pl.ds((i * wide + 64 + t) * 8 + 7, 1), :]
            wbuf[i, pl.ds(t, 1), :] = s0[pl.ds((i * wide + 4 + t) * 8, 1), :]
        return carry

    wait_bytes(cv, lsem.at[8])
    lax.fori_loop(0, rows, turn, 0, unroll=2)
    at_east, at_west = (a, lax.rem(b + 1, n_lon)), (a, lax.rem(b + n_lon - 1, n_lon))

    @pl.when(a > 0)
    def _():
        southward.wait_recv()

    @pl.when(a < n_lat - 1)
    def _():
        northward.wait_recv()

    for f, k_ref in enumerate((kl_ref, kn_ref)):
        base = 32 * f
        kx[base : base + STEPS, :] = knorth[f]
        kx[base + STEPS : base + STEPS + rows, :] = k_ref[...]
        kx[base + rows + STEPS : base + rows + 2 * STEPS, :] = ksouth[f]
        kx[base + ext : base + 32, :] = jnp.zeros((32 - ext, kx.shape[1]), F32)
    turn_coeffs(kx, kt_ref)
    for t in range(STEPS):
        kebuf[pl.ds(t, 1), :] = kt_ref[pl.ds((64 + t) * 8 + 7, 1), :]
        kwbuf[pl.ds(t, 1), :] = kt_ref[pl.ds((4 + t) * 8, 1), :]
    edges = (
        remote(ebuf, west, esem.at[0], esem.at[1], at_east),
        remote(wbuf, east, esem.at[2], esem.at[3], at_west),
        remote(kebuf, kwest, ksem2.at[0], ksem2.at[1], at_east),
        remote(kwbuf, keast, ksem2.at[2], ksem2.at[3], at_west),
    )
    for c in edges:
        c.start()

    for c in own1:
        c.wait()
    for ref, src, at in ((w1, w_ref, 0), (s1s, s_ref, 2)):
        part = pl.ds(0, n_lon - 1)
        wait_bytes(src.at[part], bulk.at[at])
        wait_bytes(ref.at[part], bulk.at[at + 1])

    def lists(t):
        return (t, jnp.maximum(t - 1, 0), jnp.minimum(t + 1, n_lat - 1))

    for step in range(1, n_lat):
        t = lat_peer(step)
        for n, of in enumerate(lists(t)):
            remote(w1.at[:, of], wo_ref.at[n, a], bulk.at[4], bulk.at[5], (t, b)).start()
            remote(s1s.at[:, of], so_ref.at[n, a], bulk.at[6], bulk.at[7], (t, b)).start()
    own2 = []
    for n, of in enumerate(lists(a)):
        own2.append(pltpu.make_async_copy(w1.at[:, of], wo_ref.at[n, a], lsem.at[2 + 2 * n]))
        own2.append(pltpu.make_async_copy(s1s.at[:, of], so_ref.at[n, a], lsem.at[3 + 2 * n]))
    for c in own2:
        c.start()

    for c in edges:
        c.wait()
    close_row(kt_ref, 0, kwest, keast, None)

    def close(i, carry):
        close_row(s0, pl.multiple_of(i * wide * 8, 8), west, east, i)
        return carry

    lax.fori_loop(0, rows, close, 0)
    spread_coeffs(kt_ref, klat, klon)
    keep = [
        pltpu.make_async_copy(klat, klat_hbm, lsem.at[9]),
        pltpu.make_async_copy(klon, klon_hbm, lsem.at[10]),
    ]
    for c in keep:
        c.start()

    def lat(q, carry):
        at = pl.ds(pl.multiple_of(q * 8, 8), 8)
        x = {STEPS + i: s0[pl.ds(pl.multiple_of((i * wide + q) * 8, 8), 8), :] for i in range(rows)}
        k = [klat[i, at, :] for i in range(ext)]
        for step in range(STEPS):
            lo, hi = min(x), max(x)
            d = {}
            for i in range(lo - 1, hi + 1):
                if i < lo:
                    d[i] = x[lo]
                elif i == hi:
                    d[i] = -x[hi]
                else:
                    d[i] = x[i + 1] - x[i]
            new = {}
            for i in range(lo - 1, hi + 2):
                if i < lo:
                    new[i] = k[i] * x[lo]
                elif i > hi:
                    new[i] = k[i] * x[hi]
                else:
                    new[i] = x[i] + k[i] * (d[i] - d[i - 1])
            x = new
        for i in range(ext):
            s1[i, at, :] = x[i]
        return carry

    lax.fori_loop(0, wide, lat, 0)

    def lon(i, carry):
        stages = [[] for _ in range(STEPS + 1)]
        diffs = [[] for _ in range(STEPS)]
        coef = []
        for q in range(wide):
            stages[0].append(s1[i, q * 8 : q * 8 + 8, :])
            coef.append(klon[i, q * 8 : q * 8 + 8, :])
            for s in range(STEPS):
                x = stages[s]
                n = len(x)
                if n >= 2:
                    diffs[s].append(x[n - 1] - x[n - 2])
                if n >= 3:
                    mid = n - 2
                    stages[s + 1].append(x[mid] + coef[mid + s] * (diffs[s][-1] - diffs[s][-2]))
                    if s == STEPS - 1:
                        field[i, mid - 1] = stages[STEPS][-1]
        pltpu.make_async_copy(field.at[i], out_hbm.at[i], lsem.at[11]).start()
        return carry

    lax.fori_loop(0, ext, lon, 0)
    wait_bytes(field, lsem.at[11])
    for c in keep:
        c.wait()
    for c in own2:
        c.wait()

    @pl.when(a < n_lat - 1)
    def _():
        southward.wait_send()

    @pl.when(a > 0)
    def _():
        northward.wait_send()

    for ref, at in ((wo_ref, 4), (so_ref, 6)):
        part = ref.at[:, pl.ds(0, n_lat - 1)]
        wait_bytes(part, bulk.at[at])
        wait_bytes(part, bulk.at[at + 1])


def forward(control4, kl, kn, wsend, ssend, n_lat, n_lon):
    rows, cols = kl.shape
    ext = rows + 2 * STEPS
    wide = 64 + 2 * STEPS
    vm = pl.BlockSpec(memory_space=pltpu.VMEM)
    hbm = pl.BlockSpec(memory_space=pl.ANY)
    edge = pltpu.VMEM((rows, STEPS, LANES), F32)
    kedge = pltpu.VMEM((STEPS, LANES), F32)
    krows = pltpu.VMEM((2, STEPS, cols), F32)
    coef = jax.ShapeDtypeStruct((ext, wide * 8, LANES), F32)
    dma = pltpu.SemaphoreType.DMA
    return pl.pallas_call(
        functools.partial(forward_kernel, n_lat, n_lon),
        out_shape=(
            jax.ShapeDtypeStruct((ext, 64, 8, LANES), F32),
            coef,
            coef,
            jax.ShapeDtypeStruct((3, n_lat, n_lon, 8, LANES), BF16),
            jax.ShapeDtypeStruct((3, n_lat, n_lon, 1, LANES), F32),
        ),
        in_specs=[hbm] + [vm] * 4,
        out_specs=(hbm, hbm, hbm, vm, vm),
        scratch_shapes=[
            pltpu.VMEM((rows * wide * 8, LANES), F32),
            pltpu.VMEM((ext, wide * 8, LANES), F32),
            pltpu.VMEM((64, cols), F32),
            pltpu.VMEM((ext, wide * 8, LANES), F32),
            pltpu.VMEM((ext, wide * 8, LANES), F32),
            pltpu.VMEM((n_lon, n_lat, 8, LANES), BF16),
            pltpu.VMEM((n_lon, n_lat, 1, LANES), F32),
            krows, krows, edge, edge, edge, edge, kedge, kedge, kedge, kedge,
            dma((8,)), dma((4,)), dma((4,)), dma((4,)), dma((12,)),
            pltpu.VMEM((control4.shape[1], 64, 8, LANES), F32),
            pltpu.VMEM((ext, 64, 8, LANES), F32),
            pltpu.VMEM((wide * 8, LANES), F32),
            pltpu.VMEM((2, 2, STEPS, cols), F32),
        ],
        compiler_params=pltpu.CompilerParams(
            vmem_limit_bytes=VMEM_BYTES, collective_id=0, has_side_effects=True),
        name="route_forward",
    )(control4, kl, kn, wsend, ssend)


def swap_kernel(n_lat, part_ref, north_ref, south_ref, sem):
    a, b = lax.axis_index("lat"), lax.axis_index("lon")
    up, down = lax.rem(a + n_lat - 1, n_lat), lax.rem(a + 1, n_lat)
    barrier = pltpu.get_barrier_semaphore()
    for t in (up, down):
        pl.semaphore_signal(barrier, inc=1, device_id=(t, b), device_id_type=MESH)
    pl.semaphore_wait(barrier, 2)
    copies = [
        remote(part_ref.at[pl.ds(0, 2)], south_ref, sem.at[0], sem.at[1], (up, b)),
        remote(part_ref.at[pl.ds(2, 2)], north_ref, sem.at[2], sem.at[3], (down, b)),
    ]
    for c in copies:
        c.start()
    for c in copies:
        c.wait()


def swap(part, n_lat):
    vm = pl.BlockSpec(memory_space=pltpu.VMEM)
    shape = jax.ShapeDtypeStruct((2,) + part.shape[1:], F32)
    return pl.pallas_call(
        functools.partial(swap_kernel, n_lat),
        out_shape=(shape, shape),
        in_specs=[vm],
        out_specs=(vm, vm),
        scratch_shapes=[pltpu.SemaphoreType.DMA((4,))],
        compiler_params=pltpu.CompilerParams(collective_id=1, has_side_effects=True),
        name="swap",
    )(part)


def rims_kernel(n_lon, west_ref, east_ref, from_west_ref, from_east_ref, sem):
    a, b = lax.axis_index("lat"), lax.axis_index("lon")
    left, right = lax.rem(b + n_lon - 1, n_lon), lax.rem(b + 1, n_lon)
    barrier = pltpu.get_barrier_semaphore()
    for t in (left, right):
        pl.semaphore_signal(barrier, inc=1, device_id=(a, t), device_id_type=MESH)
    pl.semaphore_wait(barrier, 2)
    copies = [
        remote(west_ref, from_east_ref, sem.at[0], sem.at[1], (a, left)),
        remote(east_ref, from_west_ref, sem.at[2], sem.at[3], (a, right)),
    ]
    for c in copies:
        c.start()
    for c in copies:
        c.wait()


def rims(west, east, n_lon):
    vm = pl.BlockSpec(memory_space=pltpu.VMEM)
    shape = jax.ShapeDtypeStruct(west.shape, F32)
    return pl.pallas_call(
        functools.partial(rims_kernel, n_lon),
        out_shape=(shape, shape),
        in_specs=[vm, vm],
        out_specs=(vm, vm),
        scratch_shapes=[pltpu.SemaphoreType.DMA((4,))],
        compiler_params=pltpu.CompilerParams(collective_id=2, has_side_effects=True),
        name="rims",
    )(west, east)


def mix_table(vert):
    twice = jnp.concatenate([vert, vert], 1)
    none = jnp.zeros_like(twice)
    return jnp.concatenate([jnp.concatenate([twice, none], 1), jnp.concatenate([none, twice], 1)], 0)


def mix_pieces(mix_ref):
    high, low = split(mix_table(mix_ref[...]))
    return jnp.concatenate([high, low], 0)


def unpack_weights(w_ref, n, wf):
    wf[...] = w_ref[n].astype(F32).reshape(wf.shape)


def mixed_pair(wf, p, mix):
    w = wf[pl.ds(p, wf.shape[0] // 8, stride=8), :].astype(BF16)
    return dot(jnp.concatenate([w, w], 1), mix)


def fill_spread(spread):
    for p in range(8):
        r = iota((LANES, 256), 0)
        c = iota((LANES, 256), 1)
        hit = (r < 96) & ((r & 15) == p + 8 * (c >> 7)) & (((r >> 4) & 1) == ((c >> 6) & 1))
        spread[:, p * 256 : (p + 1) * 256] = hit.astype(F32).astype(BF16)


def half_columns(x, gh):
    lane = iota(x.shape, 1)
    low = jnp.where((gh == 0) & (lane < CAP), x, 0.0)
    high = jnp.where((gh == 1) & (lane < CAP), x, 0.0)
    x = low + pltpu.roll(high, CAP, 1)
    first = x.astype(BF16).astype(F32)
    rest = x - first
    second = rest.astype(BF16).astype(F32)
    return (first + pltpu.roll(second, 32, 1) + pltpu.roll(rest - second, 64, 1)).astype(BF16)


def list_fields(s_ref, n, have):
    value = s_ref[n].reshape(-1, LANES)
    rinv = pltpu.roll(value, LANES - 16, 1)
    cell = (pltpu.roll(value, LANES - 32, 1) * 128.0 + pltpu.roll(value, LANES - 48, 1)).astype(I32)
    row = cell >> 10
    col = cell & 1023
    where = (col & 63) * 8 + ((col >> 6) & 7)
    valid = (rinv > 0.5) & (iota(value.shape, 1) < jnp.where(have[n] > 0, CAP, 0))
    return value, rinv, row, where, col >> 9, valid


def count_max(mask, weight):
    return jnp.max(jnp.where(mask, weight, 0), axis=1, keepdims=True)


def relevant(row, valid):
    return (valid, valid & (row >= 12), valid & (row < STEPS))


def tables(number, row, where, valid):
    lane = iota(row.shape, 1)
    front = valid & (row < 12)
    back = valid & (row >= 12)
    slot = lane + 1
    depth = CAP - lane
    need = relevant(row, valid)[number]
    shift = (STEPS, -12, 20)[number]
    gather = jnp.where(need, (row + shift) * 512 + where, 0)
    if number == 0:
        first = jnp.where(front, row * 512 + where, 12 * 512)
        second = jnp.where(back, (row - 12) * 512 + where, 4 * 512)
        nf = count_max(front, slot)
        nb = count_max(back, depth)
        mid = jnp.maximum(nf, nb - 4)
        late = jnp.maximum(nf - 4, nb)
        n0, n1, n2, n3 = mid, late, nf, nb
    elif number == 1:
        first = jnp.where(need, (row - 12) * 512 + where, 4 * 512)
        second = first
        n0 = n1 = n2 = n3 = count_max(need, depth)
    else:
        first = jnp.where(need, row * 512 + where, 4 * 512)
        second = first
        n0 = n1 = n2 = n3 = count_max(need, slot)
    out = jnp.where(lane < 16, gather, 0)
    out = jnp.where((lane >= 16) & (lane < 32), pltpu.roll(first, 16, 1), out)
    out = jnp.where((lane >= 32) & (lane < 48), pltpu.roll(second, 32, 1), out)
    for at, n in ((48, n0), (49, n1), (50, n2), (51, n3)):
        out = jnp.where(lane == at, n, out)
    return out


def neighbours(n_lat):
    a = lax.axis_index("lat")
    return (1, jnp.where(a > 0, 1, 0), jnp.where(a < n_lat - 1, 1, 0))


def gather_kernel(n_lat, field_hbm, mix_ref, w_ref, s_ref, part_ref, table_ref, field, picked, wf, spread, ones, smem, sem):
    devices = table_ref.shape[1]
    load = pltpu.make_async_copy(field_hbm, field, sem.at[0])
    load.start()
    have = neighbours(n_lat)
    info = []
    for n in range(3):
        value, rinv, row, where, gh, valid = list_fields(s_ref, n, have)
        table_ref[n] = tables(n, row, where, valid)
        keep = relevant(row, valid)[n]
        info.append(half_columns(jnp.where(keep, 1.0, 0.0), gh))
    copy = pltpu.make_async_copy(table_ref, smem, sem.at[1])
    copy.start()
    fill_spread(spread)
    for k in range(CAP):
        ones[k] = (iota((256, LANES), 1) == k).astype(F32).astype(BF16)
    copy.wait()
    load.wait()

    def fetch(n, s, slots):
        for k in slots:
            r = smem[n, s, k]
            picked[n, k, pl.ds(s, 1), :] = field[pl.ds(r, 1), :]

    def source(s, carry):
        fetch(0, s, range(CAP))
        fetch(1, s, (12, 13, 14, 15))
        fetch(2, s, (0, 1, 2, 3))
        north, south = smem[1, s, 48], smem[2, s, 48]

        @pl.when(jnp.maximum(north, south) > 4)
        def _():
            fetch(1, s, range(12))
            fetch(2, s, range(4, CAP))

        return carry

    lax.fori_loop(0, devices, source, 0)
    mix = mix_pieces(mix_ref)
    for n in range(3):
        unpack_weights(w_ref, n, wf)
        total = jnp.zeros((devices, LANES), F32)
        for p in range(8):
            u = mixed_pair(wf, p, mix)
            sel = dot(info[n], spread[:, p * 256 : (p + 1) * 256])
            for e in range(2):
                k = p + 8 * e
                cols = slice(e * LANES, (e + 1) * LANES)
                prod = jnp.where(sel[:, cols] > 0.5, u[:, cols] * picked[n, k], 0.0)
                total = total + dot(jnp.concatenate(list(split(prod)), 1), ones[k])
        total = total.T[:CAP]
        for at in ((0, 2), (1,), (3,))[n]:
            part_ref[at] = total


def gather(field, mix, wo, so):
    n_lat = wo.shape[1]
    devices = n_lat * wo.shape[2]
    vm = pl.BlockSpec(memory_space=pltpu.VMEM)
    return pl.pallas_call(
        functools.partial(gather_kernel, n_lat),
        out_shape=(
            jax.ShapeDtypeStruct((4, CAP, devices), F32),
            jax.ShapeDtypeStruct((3, devices, LANES), I32),
        ),
        in_specs=[pl.BlockSpec(memory_space=pl.ANY)] + [vm] * 3,
        out_specs=(vm, vm),
        scratch_shapes=[
            pltpu.VMEM(field.shape, F32),
            pltpu.VMEM((3, CAP, devices, LANES), F32),
            pltpu.VMEM((devices * 8, LANES), F32),
            pltpu.VMEM((LANES, 2048), BF16),
            pltpu.VMEM((CAP, 256, LANES), BF16),
            pltpu.SMEM((3, devices, LANES), I32),
            pltpu.SemaphoreType.DMA((2,)),
        ],
        compiler_params=pltpu.CompilerParams(vmem_limit_bytes=VMEM_BYTES),
        name="gather",
    )(field, mix, wo, so)


def adjoint_kernel(n_lat, part_ref, north_ref, south_ref, table_ref, mix_ref, w_ref, s_ref, klon_hbm, *refs):
    out_hbm, west_ref, east_ref, wf, spread, force, a_north, a_front, a_back, a_south, s1, klon, sem = refs
    devices = part_ref.shape[2]
    ext = klon.shape[0]
    rows = ext - 2 * STEPS
    load = pltpu.make_async_copy(klon_hbm, klon, sem.at[0])
    load.start()
    have = neighbours(n_lat)
    for a in (a_north, a_front, a_back, a_south):
        size = a.shape[0] // 64

        def clear(i, carry, a=a):
            a[pl.ds(pl.multiple_of(i * 64, 64), 64), :] = jnp.zeros((64, LANES), F32)
            return carry

        lax.fori_loop(0, size, clear, 0)
    fill_spread(spread)
    north = [jnp.where(have[1] > 0, north_ref[n], 0.0) for n in range(2)]
    south = [jnp.where(have[2] > 0, south_ref[n], 0.0) for n in range(2)]
    totals = (part_ref[0] + north[1] + south[1], part_ref[1] + north[0], part_ref[3] + south[0])
    blank = jnp.zeros((LANES - CAP, devices), F32)
    totals = [jnp.concatenate([t, blank], 0).T for t in totals]
    mix = mix_pieces(mix_ref)
    for n in range(3):
        unpack_weights(w_ref, n, wf)
        value, rinv, row, where, gh, valid = list_fields(s_ref, n, have)
        coef = half_columns(rinv * (totals[n] - value), gh)
        for p in range(8):
            f = mixed_pair(wf, p, mix) * dot(coef, spread[:, p * 256 : (p + 1) * 256])
            force[n, p] = f[:, :LANES]
            force[n, p + 8] = f[:, LANES:]

    def add(a, n, s, k, at):
        r = table_ref[n, s, at + k]
        a[pl.ds(r, 1), :] += force[n, k, pl.ds(s, 1), :]

    def source(s, carry):
        for k in range(4):
            add(a_front, 0, s, k, 16)
            add(a_back, 0, s, CAP - 1 - k, 32)
            add(a_north, 1, s, CAP - 1 - k, 16)
            add(a_south, 2, s, k, 16)
        nf, nb = table_ref[0, s, 50], table_ref[0, s, 51]
        north, south = table_ref[1, s, 48], table_ref[2, s, 48]
        def front(g):
            for k in range(4 * g, 4 * g + 4):
                add(a_front, 0, s, k, 16)

        @pl.when(nf > 4)
        def _():
            front(1)

            @pl.when(nf > 8)
            def _():
                front(2)
                front(3)

        @pl.when(jnp.maximum(nb, jnp.maximum(north, south)) > 4)
        def _():
            for k in range(4, CAP):
                add(a_back, 0, s, CAP - 1 - k, 32)
                add(a_north, 1, s, CAP - 1 - k, 16)
                add(a_south, 2, s, k, 16)

        return carry

    lax.fori_loop(0, devices, source, 0)
    load.wait()
    none = jnp.zeros((8, LANES), F32)

    def lon(source, first, count):
        def one(i, carry):
            stages = [{} for _ in range(STEPS + 1)]
            k = {}
            h = [{} for _ in range(STEPS)]
            d = [{} for _ in range(STEPS)]

            def coef(q):
                if q not in k:
                    k[q] = klon[first + i, (q + STEPS) * 8 : (q + STEPS) * 8 + 8, :]
                return k[q]

            for q in range(-1, 64 + 2 * STEPS + 1):
                for s in range(STEPS):
                    lo, hi = -s, 63 + s
                    at = q - s
                    if s == 0 and lo <= at <= hi:
                        stages[0][at] = source[pl.ds(pl.multiple_of((i * 64 + at) * 8, 8), 8), :]
                    if lo <= at <= hi + 2:
                        if at == lo:
                            h[s][at] = coef(at) * stages[s][at]
                            d[s][at - 1] = h[s][at]
                            stages[s + 1][at - 1] = h[s][at]
                        else:
                            if at <= hi:
                                h[s][at] = coef(at) * stages[s][at]
                            if at <= hi:
                                d[s][at - 1] = h[s][at] - h[s][at - 1]
                            elif at == hi + 1:
                                d[s][at - 1] = -h[s][at - 1]
                            m = at - 1
                            if m <= hi:
                                stages[s + 1][m] = stages[s][m] + (d[s][m] - d[s][m - 1])
                            else:
                                stages[s + 1][m] = -d[s][m - 1]
            done = stages[STEPS]
            for t in range(STEPS):
                low, high = done[t - STEPS], done[64 + t]
                west_ref[first + i, pl.ds(t, 1), :] = low[0:1]
                east_ref[first + i, pl.ds(t, 1), :] = high[GROUPS - 1 :]
                done[60 + t] = done[60 + t] + wrap_high(low, none)
                done[t] = done[t] + wrap_low(high, none)
            for q in range(64):
                s1[first + i, q * 8 : q * 8 + 8, :] = done[q]
            pltpu.make_async_copy(s1.at[first + i], out_hbm.at[first + i], sem.at[1]).start()
            return carry

        lax.fori_loop(0, count, one, 0)

    lon(a_north, 0, STEPS)
    lon(a_front, STEPS, 12)
    lon(a_back, rows, STEPS)
    lon(a_south, rows + STEPS, STEPS)

    wait_bytes(s1, sem.at[1])


def adjoint(part, north, south, table, mix, wo, so, klon):
    devices = part.shape[2]
    ext = klon.shape[0]
    vm = pl.BlockSpec(memory_space=pltpu.VMEM)
    sm = pl.BlockSpec(memory_space=pltpu.SMEM)
    hbm = pl.BlockSpec(memory_space=pl.ANY)
    edge = jax.ShapeDtypeStruct((ext, STEPS, LANES), F32)
    return pl.pallas_call(
        functools.partial(adjoint_kernel, wo.shape[1]),
        out_shape=(jax.ShapeDtypeStruct((ext, 512, LANES), F32), edge, edge),
        in_specs=[vm] * 3 + [sm] + [vm] * 3 + [hbm],
        out_specs=(hbm, vm, vm),
        scratch_shapes=[
            pltpu.VMEM((devices * 8, LANES), F32),
            pltpu.VMEM((LANES, 2048), BF16),
            pltpu.VMEM((3, CAP, devices, LANES), F32),
            pltpu.VMEM((4 * 512 + 64, LANES), F32),
            pltpu.VMEM((12 * 512 + 64, LANES), F32),
            pltpu.VMEM((4 * 512 + 64, LANES), F32),
            pltpu.VMEM((4 * 512 + 64, LANES), F32),
            pltpu.VMEM((ext, 512, LANES), F32),
            pltpu.VMEM(klon.shape, F32),
            pltpu.SemaphoreType.DMA((2,)),
        ],
        compiler_params=pltpu.CompilerParams(vmem_limit_bytes=VMEM_BYTES),
        name="adjoint_lon",
    )(part, north, south, table, mix, wo, so, klon)


def finish_kernel(field_hbm, west_ref, east_ref, klat_hbm, c_hbm, out_hbm, field, klat, cv, ov, cbuf, sem):
    ext = west_ref.shape[0]
    rows = ext - 2 * STEPS
    parts = 4
    span = 512 // parts
    pieces = []
    for c in range(parts):
        at = pl.ds(c * span, span)
        pieces.append(pltpu.make_async_copy(field_hbm.at[:, at], field.at[:, at], sem.at[c]))
        shifted = pl.ds(STEPS * 8 + c * span, span)
        pieces.append(pltpu.make_async_copy(klat_hbm.at[:, shifted], klat.at[:, at], sem.at[parts + c]))
    for c in pieces:
        c.start()
    for c in block_copies(c_hbm, cv, sem.at[2 * parts]):
        c.start()
    sub = iota((8, LANES), 0)
    lane = iota((8, LANES), 1)

    def rim(first, ref, mask):
        def one(i, carry):
            for t in range(STEPS):
                at = pl.ds((first + t) * 8, 8)
                field[i, at, :] += jnp.where(mask, edge_rows(ref, i, t), 0.0)
            return carry

        lax.fori_loop(0, ext, one, 0)

    def lat(q, carry):
        at = pl.ds(pl.multiple_of(q * 8, 8), 8)
        x = {i: field[i, at, :] for i in range(ext)}
        k = [klat[i, at, :] for i in range(ext)]
        for step in range(STEPS):
            h = {i: k[i] * x[i] for i in x}
            lo, hi = min(x), max(x)
            d = {i: h[i + 1] - h[i] for i in range(lo, hi)}
            x = {i: x[i] + (d[i] - d[i - 1]) for i in range(lo + 1, hi)}
        for i in range(rows):
            cbuf[i, at, :] = x[STEPS + i]
        return carry

    for c in range(parts):
        pieces[2 * c].wait()
        pieces[2 * c + 1].wait()
        if c == 0:
            rim(0, west_ref, (sub == 0) & (lane < 64))
        if c == parts - 1:
            rim(60, east_ref, (sub == GROUPS - 1) & (lane >= 64))
        lax.fori_loop(c * span // 8, (c + 1) * span // 8, lat, 0)
    wait_bytes(cv, sem.at[2 * parts])
    flat = cv.shape[0] * 512
    c_ref, o_ref = cv.reshape(flat, LANES), ov.reshape(flat, LANES)

    def turn(i, carry):
        for p in range(4):
            t = jnp.concatenate(
                [cbuf[i, pl.ds(2 * p, 64, stride=8), :], cbuf[i, pl.ds(2 * p + 1, 64, stride=8), :]], 0
            ).T
            for gh in range(2):
                at = tile_rows(i, 4 * gh + p)
                o_ref[at, :] = c_ref[at, :] + t[gh * 64 : gh * 64 + 64]
        return carry

    for it in range(rows // 8):
        lax.fori_loop(8 * it, 8 * it + 8, turn, 0, unroll=2)
        for b in range(8 * it, 8 * it + 8):
            pltpu.make_async_copy(ov.at[b], out_hbm.at[:, b], sem.at[2 * parts + 1]).start()
    wait_bytes(ov, sem.at[2 * parts + 1])


def finish(field, west, east, klat, control4):
    vm = pl.BlockSpec(memory_space=pltpu.VMEM)
    hbm = pl.BlockSpec(memory_space=pl.ANY)
    levels, blocks = control4.shape[:2]
    tiles = pltpu.VMEM((blocks, levels, 8, LANES), F32)
    return pl.pallas_call(
        finish_kernel,
        out_shape=jax.ShapeDtypeStruct(control4.shape, F32),
        in_specs=[hbm, vm, vm, hbm, hbm],
        out_specs=hbm,
        scratch_shapes=[
            pltpu.VMEM(field.shape, F32),
            pltpu.VMEM(field.shape, F32),
            tiles,
            tiles,
            pltpu.VMEM((field.shape[0] - 2 * STEPS, 512, LANES), F32),
            pltpu.SemaphoreType.DMA((10,)),
        ],
        compiler_params=pltpu.CompilerParams(vmem_limit_bytes=VMEM_BYTES),
        name="adjoint_lat",
    )(field, west, east, klat, control4)


def body(control, vert_sqrt, kappa_lat, kappa_lon, obs_owner, obs_cell, obs_weights, obs_value, obs_rinv, obs_count):
    levels, rows, cols = control.shape
    n_lat, n_lon = lax.axis_size("lat"), lax.axis_size("lon")
    total = obs_cell.shape[0]
    wsend, ssend = pack(
        obs_count, obs_owner.reshape(1, total), obs_cell.reshape(1, total), obs_value, obs_rinv, obs_weights, n_lat, n_lon
    )
    control4 = to_tiles(control)
    field, klat, klon, wo, so = forward(control4, kappa_lat, kappa_lon, wsend, ssend, n_lat, n_lon)
    part, table = gather(field.reshape(-1, LANES), vert_sqrt, wo, so)
    north, south = swap(part, n_lat)
    out, west_out, east_out = adjoint(part, north, south, table, vert_sqrt, wo, so, klon)
    from_west, from_east = rims(west_out, east_out, n_lon)
    return from_tiles(finish(out, from_west, from_east, klat, control4), control.shape)


def solution(mesh):
    in_specs = (
        P(None, "lat", "lon"),
        P(),
        P("lat", "lon"),
        P("lat", "lon"),
        P(("lat", "lon"), None),
        P(("lat", "lon")),
        P(None, ("lat", "lon")),
        P(("lat", "lon")),
        P(("lat", "lon")),
        P(("lat", "lon")),
    )
    out_specs = P(None, "lat", "lon")
    return jax.shard_map(body, mesh=mesh, in_specs=in_specs, out_specs=out_specs, check_vma=False)
```
